32 devices in a mesh: dp: 8 (over z, x), tensor: 4 (over y, core).
Axes of the slice: x: 2, y: 2, z: 4, core: 2. Of those that a mesh axis runs over, the one named last changes fastest.
Arguments:
- tokens: bfloat16 [4096, 2048], P(('dp', 'tensor')), may hold values from -6 to 6
- segments: int32 [8, 512], P('dp'), may hold values from 0 to 3, never falling along the last dimension, each value on 1 to 256 neighbouring positions
- expert_ids: int32 [4096, 6], P('dp'), may hold values from 0 to 63, all different within a row; in each aligned block of 512 rows (0 to 511, 512 to 1023, ...) at most 64 rows name the same one
- cotangent: bfloat16 [4096, 2048], P(('dp', 'tensor')), may hold values from -6 to 6
- attn_gain: bfloat16 [2048], P(('dp', 'tensor')), may hold values from 0.5 to 1.5
- ffn_gain: bfloat16 [2048], P(('dp', 'tensor')), may hold values from 0.5 to 1.5
- latent_gain: bfloat16 [512], P(('dp', 'tensor')), may hold values from 0.5 to 1.5
- latent_down: bfloat16 [2048, 576], P(('dp', 'tensor')), may hold values from -0.125 to 0.125
- router_proj: bfloat16 [2048, 64], P(('dp', 'tensor')), may hold values from -0.125 to 0.125
- query_proj: bfloat16 [2048, 3072], P('dp', 'tensor'), may hold values from -0.125 to 0.125
- kv_expand: bfloat16 [512, 4096], P('dp', 'tensor'), may hold values from -0.25 to 0.25
- output_proj: bfloat16 [2048, 2048], P('dp', 'tensor'), may hold values from -0.75 to 0.75
- shared_gate: bfloat16 [2048, 2816], P('dp', 'tensor'), may hold values from -0.125 to 0.125
- shared_up: bfloat16 [2048, 2816], P('dp', 'tensor'), may hold values from -0.125 to 0.125
- shared_down: bfloat16 [2048, 2816], P('dp', 'tensor'), may hold values from -0.109375 to 0.109375
- experts: bfloat16 [64, 3, 2048, 1408], P('dp', None, None, 'tensor'), may hold values from -0.125 to 0.125
Outputs:
- block_out: float32 [4096, 2048], P(('dp', 'tensor'))
- grad_tokens: float32 [4096, 2048], P(('dp', 'tensor'))
- grad_attn_gain: float32 [2048], P(('dp', 'tensor'))
- grad_ffn_gain: float32 [2048], P(('dp', 'tensor'))
- grad_latent_gain: float32 [512], P(('dp', 'tensor'))
- grad_latent_down: float32 [2048, 576], P(('dp', 'tensor'))
- grad_router: float32 [2048, 64], P(('dp', 'tensor'))
- grad_query: float32 [2048, 3072], P('dp', 'tensor')
- grad_kv_expand: float32 [512, 4096], P('dp', 'tensor')
- grad_output_proj: float32 [2048, 2048], P('dp', 'tensor')
- grad_shared_gate: float32 [2048, 2816], P('dp', 'tensor')
- grad_shared_up: float32 [2048, 2816], P('dp', 'tensor')
- grad_shared_down: float32 [2048, 2816], P('dp', 'tensor')
- grad_experts: float32 [64, 3, 2048, 1408], P('dp', None, None, 'tensor')
The draws below stay inside these ranges and needn't reach their ends.
Inputs may be any that keep to these rules, and one draw needn't show every extreme that they name: `expert_ids`: each row names 6 different experts. In each aligned block of 512 rows (one packed sequence) no expert is named by more than 64 rows, a bound that some block reaches. `segments`: along each sequence the segment numbers never fall; each document spans 1 to 256 positions, and one spans exactly that many.
All inputs are finite; a program needn't handle non-finite values.
Results may differ from the reference program's by a relative error of at most 0.025.
Values may be sent and summed in bfloat16 or wider, within the bound.
No kernel may reach another device: no remote copies, remote signals or barrier semaphores. Data moves between devices by JAX's collectives and lax.ppermute only.
A program may use at most 576 MiB of HBM per device.

```python
import math
import jax
import jax.numpy as jnp
import numpy as np
from jax import lax

D = 2048
HEADS = 16
NOPE = 128
ROPE = 64
VDIM = 128
LAT = 512
EXPERTS = 64
TOPK = 6
FF = 1408
SFF = 2816
TOK_GRP = 512
SEQS = 8
TOKENS = 4096
CAP = 64


def block_levels(stream_key, dims, split, smallest, top_value):
    level = 1.0
    for dim, parts in split:
        steps = jax.random.uniform(jax.random.fold_in(jax.random.fold_in(stream_key, 6), dim), (parts,), jnp.float32, smallest / len(split), top_value / len(split))
        level = level * jnp.repeat(jnp.exp(steps), dims[dim] // parts).reshape((-1,) + (1,) * (len(dims) - 1 - dim))
    return level


def split_up(amount, total, most, lean):
    portions = [(1 << 20) // math.isqrt(standing ** lean) + 1 for standing in range(2, amount + 1)]
    spare, given = total - most - (amount - 1), [1] * (amount - 1)
    while spare > 0:
        movable = [i for i in range(amount - 1) if given[i] < most]
        mass, left = sum([portions[i] for i in movable]), spare
        for i in movable:
            more = min(most - given[i], max(1, left * portions[i] // mass), spare)
            given[i] = given[i] + more
            spare = spare - more
    return np.array([most] + given)


def ragged(key, amount, total, most, skew):
    if amount == 2:
        one = jax.random.randint(key, (), max(1, total - most), min(most, total - 1) + 1)
        return jnp.stack([one, total - one])
    tallies = jnp.asarray(split_up(amount, total, most, skew), jnp.int32)
    pairs = (amount - 1) // 2
    donor, receiver = tallies[1:1 + 2 * pairs:2], tallies[2:2 + 2 * pairs:2]
    slack = jnp.minimum(donor - 1, most - receiver)
    passed = jax.random.randint(jax.random.fold_in(key, 1), (pairs,), 0, 1 << 20) % (slack + 1)
    tallies = tallies.at[1:1 + 2 * pairs:2].set(donor - passed).at[2:2 + 2 * pairs:2].set(receiver + passed)
    return tallies[jax.random.permutation(jax.random.fold_in(key, 2), amount)]


def deal_out(rng, own, number, rows, amount, top, reach, skew):
    order = jax.random.permutation(rng, amount)
    crowded, usual = load_shares(amount, rows * top, reach, skew, True), load_shares(amount, rows * top, reach, skew, False)
    places = jnp.arange(amount)

    def named(lengths, offset_by):
        used = int((lengths > 0).sum())
        fixed = max(1, used // 4)
        moved = fixed + (places - fixed + offset_by * (used - fixed)) % max(1, amount - fixed)
        return jnp.zeros((amount,), jnp.int32).at[order[jnp.where(places < fixed, places, moved)]].set(jnp.asarray(lengths, jnp.int32))

    lengths = jnp.where(number % 4 == 0, named(crowded, number // 4), named(usual, number - number // 4 - 1))
    mixed = jax.random.permutation(jax.random.fold_in(own, 3), amount)
    source_of, sink = mixed[0:amount // 2 * 2:2], mixed[1:amount // 2 * 2:2]
    margin = jnp.minimum(lengths[source_of] - 1, reach - lengths[sink]) // 2
    margin = jnp.where((source_of == order[0]) | (sink == order[0]) | (lengths[sink] == 0), 0, jnp.maximum(margin, 0))
    moved = jax.random.randint(jax.random.fold_in(own, 4), (amount // 2,), 0, 1 << 20) % (margin + 1)
    lengths = lengths.at[source_of].add(-moved).at[sink].add(moved)
    items = jnp.searchsorted(jnp.cumsum(lengths), jnp.arange(rows * top), side="right").astype(jnp.int32)
    grid = items.reshape(top, rows).T
    grid = grid[jax.random.permutation(jax.random.fold_in(own, 1), rows)]
    offset_by = jax.random.randint(jax.random.fold_in(own, 2), (rows, 1), 0, top)
    return jnp.take_along_axis(grid, (jnp.arange(top)[None, :] + offset_by) % top, axis=1)


def load_shares(amount, total, bound, lean, full):
    loads = [(1 << 20) // math.isqrt(standing ** lean) + 1 for standing in range(1, amount + 1)]
    largest = bound if full else min(bound, max(-(-total // amount), total * loads[0] // sum(loads)))
    least = 1 if total - largest >= amount - 1 else 0
    counts, rest = [largest] + [least] * (amount - 1), total - largest - least * (amount - 1)
    while rest > 0:
        candidates = [i for i in range(1, amount) if counts[i] < largest] or [i for i in range(1, amount) if counts[i] < bound]
        pool, budget = sum([loads[i] for i in candidates]), rest
        for i in candidates:
            extra = min(bound - counts[i], max(1, budget * loads[i] // pool), rest)
            counts[i] = counts[i] + extra
            rest = rest - extra
    return np.array(counts)


def noise(key, dims, spread, limit, shards=(), kind=jnp.bfloat16):
    loudness = block_levels(key, dims, shards, -0.22, 0.18) if shards else 1.0
    entries = jax.random.normal(key, dims, jnp.float32) * spread * loudness
    return jnp.minimum(jnp.maximum(entries, -limit), limit).astype(kind)


def setup_inputs(seed: int = 0) -> dict:
    streams_of = jax.random.split(jax.random.key(seed), 17)
    tokens = noise(streams_of[0], (TOKENS, D), 1.0, 6.0, ((0, 32),))
    segments = jax.vmap(lambda own: jnp.searchsorted(jnp.cumsum(ragged(own, 4, TOK_GRP, TOK_GRP // 2, 0)), jnp.arange(TOK_GRP), side="right"))(jax.random.split(streams_of[1], SEQS)).reshape((SEQS, TOK_GRP)).astype(jnp.int32)
    expert_ids_keys = jax.random.split(jax.random.fold_in(streams_of[2], 1), TOKENS // TOK_GRP)
    expert_ids_turns = jax.random.permutation(jax.random.fold_in(streams_of[2], 3), TOKENS // TOK_GRP)
    expert_ids = jax.vmap(lambda own, number: deal_out(jax.random.fold_in(streams_of[2], 2), own, number, TOK_GRP, EXPERTS, TOPK, CAP, 1))(expert_ids_keys, expert_ids_turns).reshape((TOKENS, TOPK))
    cotangent = noise(streams_of[3], (TOKENS, D), 1.0, 6.0, ((0, 32),))
    attn_gain = jnp.clip(1.0 + 0.1 * jax.random.normal(streams_of[4], (D,), jnp.float32), 0.5, 1.5).astype(jnp.bfloat16)
    ffn_gain = jnp.clip(1.0 + 0.1 * jax.random.normal(streams_of[5], (D,), jnp.float32), 0.5, 1.5).astype(jnp.bfloat16)
    latent_gain = jnp.clip(1.0 + 0.1 * jax.random.normal(streams_of[6], (LAT,), jnp.float32), 0.5, 1.5).astype(jnp.bfloat16)
    latent_down = noise(streams_of[7], (D, LAT + ROPE), D ** -0.5, 0.125, ((0, 32),))
    router_proj = noise(streams_of[8], (D, EXPERTS), D ** -0.5, 0.125, ((0, 32),))
    query_proj = noise(streams_of[9], (D, HEADS * (NOPE + ROPE)), D ** -0.5, 0.125, ((0, 8), (1, 4)))
    kv_expand = noise(streams_of[10], (LAT, HEADS * (NOPE + VDIM)), LAT ** -0.5, 0.25, ((0, 8), (1, 4)))
    output_proj = noise(streams_of[11], (D, HEADS * VDIM), (HEADS * VDIM // 32) ** -0.5, 0.75, ((0, 8), (1, 4)))
    shared_gate = noise(streams_of[12], (D, SFF), D ** -0.5, 0.125, ((0, 8), (1, 4)))
    shared_up = noise(streams_of[13], (D, SFF), D ** -0.5, 0.125, ((0, 8), (1, 4)))
    shared_down = noise(streams_of[14], (D, SFF), SFF ** -0.5, 0.109375, ((0, 8), (1, 4)))
    experts = noise(streams_of[15], (EXPERTS, 3, D, FF), D ** -0.5, 0.125, ((0, 8), (3, 4)))
    return dict(tokens=tokens, segments=segments, expert_ids=expert_ids, cotangent=cotangent, attn_gain=attn_gain, ffn_gain=ffn_gain, latent_gain=latent_gain, latent_down=latent_down, router_proj=router_proj, query_proj=query_proj, kv_expand=kv_expand, output_proj=output_proj, shared_gate=shared_gate, shared_up=shared_up, shared_down=shared_down, experts=experts)


eps = 1e-06
route_scale = 2.446
rope_base = 50000.0

def rms_scale(values):
    return lax.rsqrt(lax.optimization_barrier(jnp.mean(values * values, axis=-1, keepdims=True)) + eps)

def norm_back(grad_normed, values, inverse, gain):
    scaled = grad_normed * gain
    return inverse * scaled - values * inverse * inverse * inverse * lax.optimization_barrier(jnp.mean(scaled * values, axis=-1, keepdims=True))

def rope_tables(count, width):
    half = width // 2
    powers = jnp.arange(half, dtype=jnp.int32).astype(jnp.float32) * (2.0 / width)
    freqs = jnp.exp(-math.log(rope_base) * powers)
    angles = jnp.arange(count, dtype=jnp.int32).astype(jnp.float32)[:, None] * freqs[None, :]
    return (jnp.cos(angles), jnp.sin(angles))

def rotate(values, cosines, sines):
    half = values.shape[-1] // 2
    first = values[..., :half]
    second = values[..., half:]
    return jnp.concatenate([first * cosines - second * sines, second * cosines + first * sines], axis=-1)

def unrotate(grads, cosines, sines):
    half = grads.shape[-1] // 2
    first = grads[..., :half]
    second = grads[..., half:]
    return jnp.concatenate([first * cosines + second * sines, second * cosines - first * sines], axis=-1)

def rounded(values):
    return lax.optimization_barrier(values.astype(jnp.bfloat16)).astype(jnp.float32)

def slots_of(route_ids, capacity):
    flat = route_ids.reshape(-1)
    onehot = (flat[:, None] == jnp.arange(EXPERTS, dtype=jnp.int32)[None, :]).astype(jnp.int32)
    earlier = jnp.cumsum(onehot, axis=0) - onehot
    position = lax.optimization_barrier(jnp.sum(earlier * onehot, axis=1)).astype(jnp.int32)
    return (flat * capacity + position).astype(jnp.int32)

def sources_of(slot, filled, total):
    return jnp.full((total,), filled, dtype=jnp.int32).at[slot].set(jnp.arange(filled, dtype=jnp.int32))

def attend(query_all, key_all, value_all, doc_ids):
    count = query_all.shape[0]
    block = min(512, count)
    scale = 1.0 / math.sqrt(query_all.shape[-1])
    key_pos = jnp.arange(count, dtype=jnp.int32)
    keys_f = key_all.astype(jnp.float32)
    values_f = value_all.astype(jnp.float32)

    def one_block(begin):
        queries = lax.dynamic_slice_in_dim(query_all, begin, block, 0).astype(jnp.float32)
        query_docs = lax.dynamic_slice_in_dim(doc_ids, begin, block, 0)
        query_pos = begin + jnp.arange(block, dtype=jnp.int32)
        allowed = (query_docs[:, None] == doc_ids[None, :]) & (key_pos[None, :] <= query_pos[:, None])
        scores = jnp.einsum('qhc,khc->hqk', queries, keys_f) * scale
        raw_weights = jnp.where(allowed[None], jnp.exp(scores), 0.0)
        total = lax.optimization_barrier(jnp.sum(raw_weights, axis=-1))
        probs = rounded(raw_weights / total[..., None])
        context = jnp.einsum('hqk,khc->qhc', probs, values_f)
        return (context, jnp.log(total))
    begins = jnp.arange(0, count, block, dtype=jnp.int32)
    contexts, logs = lax.map(one_block, begins)
    heads = query_all.shape[1]
    context = contexts.reshape((count, heads, value_all.shape[2]))
    log_total = jnp.transpose(logs, (1, 0, 2)).reshape((heads, count))
    return (context, log_total)

def attend_back(query_all, key_all, value_all, doc_ids, log_total, d_context):
    count = query_all.shape[0]
    heads = query_all.shape[1]
    block = min(512, count)
    scale = 1.0 / math.sqrt(query_all.shape[-1])
    key_pos = jnp.arange(count, dtype=jnp.int32)
    keys_f = key_all.astype(jnp.float32)
    values_f = value_all.astype(jnp.float32)

    def one_block(carry, begin):
        d_keys, d_values = carry
        queries = lax.dynamic_slice_in_dim(query_all, begin, block, 0).astype(jnp.float32)
        query_docs = lax.dynamic_slice_in_dim(doc_ids, begin, block, 0)
        query_pos = begin + jnp.arange(block, dtype=jnp.int32)
        allowed = (query_docs[:, None] == doc_ids[None, :]) & (key_pos[None, :] <= query_pos[:, None])
        scores = jnp.einsum('qhc,khc->hqk', queries, keys_f) * scale
        logs = lax.dynamic_slice_in_dim(log_total, begin, block, 1)
        probs = jnp.where(allowed[None], jnp.exp(scores - logs[..., None]), 0.0)
        grads = lax.dynamic_slice_in_dim(d_context, begin, block, 0).astype(jnp.float32)
        d_values = d_values + jnp.einsum('hqk,qhc->khc', rounded(probs), grads)
        d_probs = jnp.einsum('qhc,khc->hqk', grads, values_f)
        delta = lax.optimization_barrier(jnp.sum(probs * d_probs, axis=-1, keepdims=True))
        d_scores = rounded(probs * (d_probs - delta) * scale)
        d_queries = jnp.einsum('hqk,khc->qhc', d_scores, keys_f)
        d_keys = d_keys + jnp.einsum('hqk,qhc->khc', d_scores, queries)
        return ((d_keys, d_values), d_queries)
    begins = jnp.arange(0, count, block, dtype=jnp.int32)
    start_state = (jnp.zeros(key_all.shape, jnp.float32), jnp.zeros(value_all.shape, jnp.float32))
    (d_keys, d_values), d_queries = lax.scan(one_block, start_state, begins)
    return (d_queries.reshape((count, heads, query_all.shape[2])), d_keys, d_values)

def reference(tokens, segments, expert_ids, cotangent, attn_gain, ffn_gain, latent_gain, latent_down, router_proj, query_proj, kv_expand, output_proj, shared_gate, shared_up, shared_down, experts):
    width_q = NOPE + ROPE
    slots_total = EXPERTS * CAP
    cosines, sines = rope_tables(TOK_GRP, ROPE)
    gain_one = attn_gain.astype(jnp.float32)
    gain_two = ffn_gain.astype(jnp.float32)
    gain_lat = latent_gain.astype(jnp.float32)

    def one_group(carry, inputs):
        rows, doc_ids, route_ids, grad_in = inputs
        acc_gain_one, acc_gain_two, acc_gain_lat, acc_down, acc_router, acc_query, acc_expand, acc_out, acc_sgate, acc_sup, acc_sdown, acc_experts = carry
        residual = rows.astype(jnp.float32)
        inv_one = rms_scale(residual)
        normed_one = (residual * inv_one * gain_one).astype(jnp.bfloat16)
        query = jnp.dot(normed_one, query_proj, preferred_element_type=jnp.float32).reshape((TOK_GRP, HEADS, width_q))
        latent = jnp.dot(normed_one, latent_down, preferred_element_type=jnp.float32)
        compressed = latent[:, :LAT]
        inv_lat = rms_scale(compressed)
        comp_normed = (compressed * inv_lat * gain_lat).astype(jnp.bfloat16)
        expanded = jnp.dot(comp_normed, kv_expand, preferred_element_type=jnp.float32).reshape((TOK_GRP, HEADS, NOPE + VDIM))
        query_rot = rotate(query[:, :, NOPE:], cosines[:, None, :], sines[:, None, :])
        key_rot = rotate(latent[:, LAT:], cosines, sines)
        query_all = jnp.concatenate([query[:, :, :NOPE], query_rot], axis=-1).astype(jnp.bfloat16)
        key_all = jnp.concatenate([expanded[:, :, :NOPE], jnp.broadcast_to(key_rot[:, None, :], (TOK_GRP, HEADS, ROPE))], axis=-1).astype(jnp.bfloat16)
        value_all = expanded[:, :, NOPE:].astype(jnp.bfloat16)
        context, log_total = attend(query_all, key_all, value_all, doc_ids)
        context_b = context.reshape((TOK_GRP, HEADS * VDIM)).astype(jnp.bfloat16)
        middle = residual + jnp.dot(context_b, output_proj.T, preferred_element_type=jnp.float32)
        inv_two = rms_scale(middle)
        normed_two = (middle * inv_two * gain_two).astype(jnp.bfloat16)
        route_scores = jax.nn.sigmoid(jnp.dot(normed_two, router_proj, preferred_element_type=jnp.float32))
        chosen = jnp.take_along_axis(route_scores, route_ids, axis=1)
        chosen_total = lax.optimization_barrier(jnp.sum(chosen, axis=1, keepdims=True))
        weights = route_scale * chosen / chosen_total
        shared_pre_gate = jnp.dot(normed_two, shared_gate, preferred_element_type=jnp.float32)
        shared_pre_up = jnp.dot(normed_two, shared_up, preferred_element_type=jnp.float32)
        shared_hidden = (jax.nn.silu(shared_pre_gate) * shared_pre_up).astype(jnp.bfloat16)
        slot = slots_of(route_ids, CAP)
        source = sources_of(slot, TOK_GRP * TOPK, slots_total)
        padded_rows = jnp.concatenate([normed_two, jnp.zeros((1, D), jnp.bfloat16)], axis=0)
        dispatched = jnp.take(padded_rows, source // TOPK, axis=0).reshape((EXPERTS, CAP, D))
        grad_rows = grad_in.astype(jnp.float32)
        scaled = (weights[:, :, None] * grad_rows[:, None, :]).astype(jnp.bfloat16).reshape((TOK_GRP * TOPK, D))
        padded_grads = jnp.concatenate([scaled, jnp.zeros((1, D), jnp.bfloat16)], axis=0)
        grads_disp = jnp.take(padded_grads, source, axis=0).reshape((EXPERTS, CAP, D))

        def expert_step(index, state):
            outs_all, backs_all, grads_all = state
            gate_w = experts[index, 0]
            up_w = experts[index, 1]
            down_w = experts[index, 2]
            inputs_e = dispatched[index]
            grads_e = grads_disp[index]
            gate_v = jnp.dot(inputs_e, gate_w, preferred_element_type=jnp.float32)
            up_v = jnp.dot(inputs_e, up_w, preferred_element_type=jnp.float32)
            hidden = (jax.nn.silu(gate_v) * up_v).astype(jnp.bfloat16)
            outs_e = jnp.dot(hidden, down_w.T, preferred_element_type=jnp.float32)
            d_hidden = jnp.dot(grads_e, down_w, preferred_element_type=jnp.float32)
            sigma_gate = jax.nn.sigmoid(gate_v)
            d_gate = (d_hidden * up_v * sigma_gate * (1.0 + gate_v * (1.0 - sigma_gate))).astype(jnp.bfloat16)
            d_up = (d_hidden * gate_v * sigma_gate).astype(jnp.bfloat16)
            grad_e = jnp.stack([jnp.dot(inputs_e.T, d_gate, preferred_element_type=jnp.float32), jnp.dot(inputs_e.T, d_up, preferred_element_type=jnp.float32), jnp.dot(grads_e.T, hidden, preferred_element_type=jnp.float32)])
            back_e = jnp.dot(d_gate, gate_w.T, preferred_element_type=jnp.float32) + jnp.dot(d_up, up_w.T, preferred_element_type=jnp.float32)
            return (outs_all.at[index].set(outs_e), backs_all.at[index].set(back_e), grads_all.at[index].add(grad_e))
        start_state = (jnp.zeros((EXPERTS, CAP, D), jnp.float32), jnp.zeros((EXPERTS, CAP, D), jnp.float32), acc_experts)
        outs_all, backs_all, acc_experts = lax.fori_loop(0, EXPERTS, expert_step, start_state)
        picked = jnp.take(outs_all.reshape((slots_total, D)), slot, axis=0).reshape((TOK_GRP, TOPK, D))
        routed = lax.optimization_barrier(jnp.sum(weights[:, :, None] * picked, axis=1))
        shared_out = jnp.dot(shared_hidden, shared_down.T, preferred_element_type=jnp.float32)
        block_out = middle + shared_out + routed
        d_weight = lax.optimization_barrier(jnp.sum(grad_rows[:, None, :] * picked, axis=-1))
        d_shared = jnp.dot(grad_in, shared_down, preferred_element_type=jnp.float32)
        sigma_shared = jax.nn.sigmoid(shared_pre_gate)
        d_sgate = (d_shared * shared_pre_up * sigma_shared * (1.0 + shared_pre_gate * (1.0 - sigma_shared))).astype(jnp.bfloat16)
        d_sup = (d_shared * shared_pre_gate * sigma_shared).astype(jnp.bfloat16)
        acc_sgate = acc_sgate + jnp.dot(normed_two.T, d_sgate, preferred_element_type=jnp.float32)
        acc_sup = acc_sup + jnp.dot(normed_two.T, d_sup, preferred_element_type=jnp.float32)
        acc_sdown = acc_sdown + jnp.dot(grad_in.T, shared_hidden, preferred_element_type=jnp.float32)
        d_chosen = route_scale * (d_weight / chosen_total - lax.optimization_barrier(jnp.sum(d_weight * chosen, axis=1, keepdims=True)) / (chosen_total * chosen_total))
        onehot = (route_ids[:, :, None] == jnp.arange(EXPERTS, dtype=jnp.int32)[None, None, :]).astype(jnp.float32)
        d_logits = (lax.optimization_barrier(jnp.sum(d_chosen[:, :, None] * onehot, axis=1)) * route_scores * (1.0 - route_scores)).astype(jnp.bfloat16)
        acc_router = acc_router + jnp.dot(normed_two.T, d_logits, preferred_element_type=jnp.float32)
        d_routed = lax.optimization_barrier(jnp.sum(jnp.take(backs_all.reshape((slots_total, D)), slot, axis=0).reshape((TOK_GRP, TOPK, D)), axis=1))
        d_normed_two = d_routed + jnp.dot(d_sgate, shared_gate.T, preferred_element_type=jnp.float32) + jnp.dot(d_sup, shared_up.T, preferred_element_type=jnp.float32) + jnp.dot(d_logits, router_proj.T, preferred_element_type=jnp.float32)
        acc_gain_two = acc_gain_two + lax.optimization_barrier(jnp.sum(d_normed_two * middle * inv_two, axis=0))
        d_middle = grad_rows + norm_back(d_normed_two, middle, inv_two, gain_two)
        d_mid_b = d_middle.astype(jnp.bfloat16)
        acc_out = acc_out + jnp.dot(d_mid_b.T, context_b, preferred_element_type=jnp.float32)
        d_context = jnp.dot(d_mid_b, output_proj, preferred_element_type=jnp.float32).astype(jnp.bfloat16).reshape((TOK_GRP, HEADS, VDIM))
        d_query, d_key, d_value = attend_back(query_all, key_all, value_all, doc_ids, log_total, d_context)
        d_query_rot = unrotate(d_query[:, :, NOPE:], cosines[:, None, :], sines[:, None, :])
        d_query_all = jnp.concatenate([d_query[:, :, :NOPE], d_query_rot], axis=-1).reshape((TOK_GRP, HEADS * width_q)).astype(jnp.bfloat16)
        acc_query = acc_query + jnp.dot(normed_one.T, d_query_all, preferred_element_type=jnp.float32)
        d_expanded = jnp.concatenate([d_key[:, :, :NOPE], d_value], axis=-1).reshape((TOK_GRP, HEADS * (NOPE + VDIM))).astype(jnp.bfloat16)
        acc_expand = acc_expand + jnp.dot(comp_normed.T, d_expanded, preferred_element_type=jnp.float32)
        d_comp_normed = jnp.dot(d_expanded, kv_expand.T, preferred_element_type=jnp.float32)
        d_key_rot = lax.optimization_barrier(jnp.sum(d_key[:, :, NOPE:], axis=1))
        acc_gain_lat = acc_gain_lat + lax.optimization_barrier(jnp.sum(d_comp_normed * compressed * inv_lat, axis=0))
        d_comp = norm_back(d_comp_normed, compressed, inv_lat, gain_lat)
        d_latent = jnp.concatenate([d_comp, unrotate(d_key_rot, cosines, sines)], axis=-1).astype(jnp.bfloat16)
        acc_down = acc_down + jnp.dot(normed_one.T, d_latent, preferred_element_type=jnp.float32)
        d_normed_one = jnp.dot(d_query_all, query_proj.T, preferred_element_type=jnp.float32) + jnp.dot(d_latent, latent_down.T, preferred_element_type=jnp.float32)
        acc_gain_one = acc_gain_one + lax.optimization_barrier(jnp.sum(d_normed_one * residual * inv_one, axis=0))
        grad_tokens = d_middle + norm_back(d_normed_one, residual, inv_one, gain_one)
        new_carry = (acc_gain_one, acc_gain_two, acc_gain_lat, acc_down, acc_router, acc_query, acc_expand, acc_out, acc_sgate, acc_sup, acc_sdown, acc_experts)
        return (new_carry, (block_out, grad_tokens))
    start_carry = (jnp.zeros((D,), jnp.float32), jnp.zeros((D,), jnp.float32), jnp.zeros((LAT,), jnp.float32), jnp.zeros((D, LAT + ROPE), jnp.float32), jnp.zeros((D, EXPERTS), jnp.float32), jnp.zeros((D, HEADS * width_q), jnp.float32), jnp.zeros((LAT, HEADS * (NOPE + VDIM)), jnp.float32), jnp.zeros((D, HEADS * VDIM), jnp.float32), jnp.zeros((D, SFF), jnp.float32), jnp.zeros((D, SFF), jnp.float32), jnp.zeros((D, SFF), jnp.float32), jnp.zeros((EXPERTS, 3, D, FF), jnp.float32))
    inputs = (tokens.reshape((SEQS, TOK_GRP, D)), segments, expert_ids.reshape((SEQS, TOK_GRP, TOPK)), cotangent.reshape((SEQS, TOK_GRP, D)))
    final, (outs, grads_in) = lax.scan(one_group, start_carry, inputs)
    return (outs.reshape((TOKENS, D)), grads_in.reshape((TOKENS, D)), final[0], final[1], final[2], final[3], final[4], final[5], final[6], final[7], final[8], final[9], final[10], final[11])
```

```python
import math

import jax
import jax.numpy as jnp
from jax import lax
from jax.experimental import pallas as pl
from jax.experimental.pallas import tpu as pltpu
from jax.sharding import PartitionSpec as P

NOPE = 128
ROPE = 64
VDIM = 128
LAT = 512
EXPERTS = 64
TOPK = 6


eps = 1e-06
route_scale = 2.446
rope_base = 50000.0


def rms_scale(values):
    return lax.rsqrt(jnp.mean(values * values, axis=-1, keepdims=True) + eps)


def norm_back(grad_normed, values, inverse, gain):
    scaled = grad_normed * gain
    return inverse * scaled - values * inverse * inverse * inverse * jnp.mean(
        scaled * values, axis=-1, keepdims=True
    )


def rope_tables(count, width):
    half = width // 2
    powers = jnp.arange(half, dtype=jnp.int32).astype(jnp.float32) * (2.0 / width)
    freqs = jnp.exp(-math.log(rope_base) * powers)
    angles = jnp.arange(count, dtype=jnp.int32).astype(jnp.float32)[:, None] * freqs[None, :]
    return (jnp.cos(angles), jnp.sin(angles))


def rotate(values, cosines, sines):
    half = values.shape[-1] // 2
    first = values[..., :half]
    second = values[..., half:]
    return jnp.concatenate(
        [first * cosines - second * sines, second * cosines + first * sines], axis=-1
    )


def unrotate(grads, cosines, sines):
    half = grads.shape[-1] // 2
    first = grads[..., :half]
    second = grads[..., half:]
    return jnp.concatenate(
        [first * cosines + second * sines, second * cosines - first * sines], axis=-1
    )


def matmul_t(left, right):
    return lax.dot_general(
        left, right, (((1,), (1,)), ((), ())), preferred_element_type=jnp.float32
    )


def matmul_tl(left, right):
    return lax.dot_general(
        left, right, (((0,), (0,)), ((), ())), preferred_element_type=jnp.float32
    )


def attend(query_all, key_all, value_all, doc_ids):
    count = query_all.shape[0]
    block = min(512, count)
    scale = 1.0 / math.sqrt(query_all.shape[-1])
    key_pos = jnp.arange(count, dtype=jnp.int32)

    def one_block(begin):
        query_pos = begin + jnp.arange(block, dtype=jnp.int32)
        allowed = (doc_ids[:, None] == doc_ids[None, :]) & (key_pos[None, :] <= query_pos[:, None])
        scores = (
            jnp.einsum("qhc,khc->hqk", query_all, key_all, preferred_element_type=jnp.float32)
            * scale
        )
        raw_weights = jnp.where(allowed[None], jnp.exp(scores), 0.0)
        total = jnp.sum(raw_weights, axis=-1)
        probs = (raw_weights / total[..., None]).astype(jnp.bfloat16)
        context = jnp.einsum("hqk,khc->qhc", probs, value_all, preferred_element_type=jnp.float32)
        return (context, jnp.log(total))

    begins = jnp.arange(0, count, block, dtype=jnp.int32)
    contexts, logs = lax.map(one_block, begins)
    heads = query_all.shape[1]
    context = contexts.reshape((count, heads, value_all.shape[2]))
    log_total = jnp.transpose(logs, (1, 0, 2)).reshape((heads, count))
    return (context, log_total)


def attend_back(query_all, key_all, value_all, doc_ids, log_total, d_context):
    count = query_all.shape[0]
    heads = query_all.shape[1]
    block = min(512, count)
    scale = 1.0 / math.sqrt(query_all.shape[-1])
    key_pos = jnp.arange(count, dtype=jnp.int32)

    def one_block(carry, begin):
        d_keys, d_values = carry
        query_pos = begin + jnp.arange(block, dtype=jnp.int32)
        allowed = (doc_ids[:, None] == doc_ids[None, :]) & (key_pos[None, :] <= query_pos[:, None])
        scores = (
            jnp.einsum("qhc,khc->hqk", query_all, key_all, preferred_element_type=jnp.float32)
            * scale
        )
        probs = jnp.where(allowed[None], jnp.exp(scores - log_total[..., None]), 0.0)
        d_values = d_values + jnp.einsum(
            "hqk,qhc->khc",
            probs.astype(jnp.bfloat16),
            d_context,
            preferred_element_type=jnp.float32,
        )
        d_probs = jnp.einsum(
            "qhc,khc->hqk", d_context, value_all, preferred_element_type=jnp.float32
        )
        delta = jnp.sum(probs * d_probs, axis=-1, keepdims=True)
        d_scores = (probs * (d_probs - delta) * scale).astype(jnp.bfloat16)
        d_queries = jnp.einsum(
            "hqk,khc->qhc", d_scores, key_all, preferred_element_type=jnp.float32
        )
        d_keys = d_keys + jnp.einsum(
            "hqk,qhc->khc", d_scores, query_all, preferred_element_type=jnp.float32
        )
        return ((d_keys, d_values), d_queries)

    begins = jnp.arange(0, count, block, dtype=jnp.int32)
    start_state = (jnp.zeros(key_all.shape, jnp.float32), jnp.zeros(value_all.shape, jnp.float32))
    (d_keys, d_values), d_queries = lax.scan(one_block, start_state, begins)
    return (d_queries.reshape((count, heads, query_all.shape[2])), d_keys, d_values)


BF = jnp.bfloat16
F32 = jnp.float32


def factor_pairs(size, stride, parts, shift):
    pairs = []
    for index in range(size):
        place = index // stride % parts
        pairs.append((index, index + ((place + shift) % parts - place) * stride))
    return pairs


def pick(array, index, dim):
    return lax.dynamic_index_in_dim(array, index, dim, keepdims=False)


def scatter_factor(array, dim, axis, stride, parts, final=False):
    size = lax.axis_size(axis)
    place = lax.axis_index(axis) // stride % parts
    received = [
        lax.ppermute(
            pick(array, (place + shift) % parts, dim),
            axis,
            factor_pairs(size, stride, parts, shift),
        )
        for shift in range(1, parts)
    ]
    total = pick(array, place, dim).astype(F32)
    for item in received:
        total = total + item.astype(F32)
    return total if final else total.astype(BF)


def factors(axis):
    size = lax.axis_size(axis)
    inner = 2 if size % 2 == 0 else 1
    return size // inner, inner


def gather_pieces(shard, axis):
    size = lax.axis_size(axis)
    outer, inner = factors(axis)
    index = lax.axis_index(axis)
    far, near = index // inner, index % inner
    pieces = [shard] + [
        lax.ppermute(shard, axis, factor_pairs(size, inner, outer, shift))
        for shift in range(1, outer)
    ]
    found = []
    for shift, piece in enumerate(pieces):
        source = (far - shift) % outer
        found.append((source, near, piece))
        for turn in range(1, inner):
            other = lax.ppermute(piece, axis, factor_pairs(size, 1, inner, turn))
            found.append((source, (near - turn) % inner, other))
    return found


def gather_rows(shard, axis):
    inner = factors(axis)[1]
    rows = shard.shape[0]
    full = jnp.zeros((lax.axis_size(axis) * rows,) + shard.shape[1:], shard.dtype)
    rest = (0,) * (shard.ndim - 1)
    for far, near, piece in gather_pieces(shard, axis):
        full = lax.dynamic_update_slice(full, piece, ((far * inner + near) * rows,) + rest)
    return full


def gather_columns(shard, axis):
    inner = factors(axis)[1]
    rows, columns = shard.shape
    full = jnp.zeros((rows, lax.axis_size(axis) * columns), shard.dtype)
    for far, near, piece in gather_pieces(shard, axis):
        full = lax.dynamic_update_slice(full, piece, (0, (far * inner + near) * columns))
    return full


def scatter_rows(array, axis, final=True):
    outer, inner = factors(axis)
    rows = array.shape[0] // (outer * inner)
    view = array.astype(BF).reshape((outer, inner, rows) + array.shape[1:])
    view = scatter_factor(view, 1, axis, 1, inner)
    return scatter_factor(view, 0, axis, inner, outer, final)


def scatter_products(lefts, rights, axis):
    size = lax.axis_size(axis)
    outer, inner = factors(axis)
    near = lax.axis_index(axis) % inner
    columns = rights[0].shape[1] // size

    def blocks(which):
        made = []
        for far in range(outer):
            begin = (far * inner + which) * columns
            made.append(
                jnp.concatenate(
                    [
                        matmul_tl(left, lax.dynamic_slice_in_dim(right, begin, columns, 1)).astype(BF)
                        for left, right in zip(lefts, rights)
                    ],
                    axis=0,
                )
            )
        return jnp.stack(made)

    sent = [
        lax.ppermute(blocks((near + turn) % inner), axis, factor_pairs(size, 1, inner, turn))
        for turn in range(1, inner)
    ]
    total = blocks(near)
    if sent:
        total = total.astype(F32)
        for item in sent:
            total = total + item.astype(F32)
        total = total.astype(BF)
    return scatter_factor(total, 0, axis, inner, outer, True)


def dot_nn(left, right):
    return lax.dot_general(left, right, (((1,), (0,)), ((), ())), preferred_element_type=F32)


def place_of(position_ref, capacity):
    _, count, tokens = position_ref.shape
    slot = lax.broadcasted_iota(jnp.int32, (capacity, tokens), 0).astype(F32)
    return jnp.concatenate(
        [
            jnp.where(position_ref[0, e : e + 1, :] == slot, 1.0, 0.0).astype(BF)
            for e in range(count)
        ],
        axis=0,
    )


def dispatch_kernel(position_ref, rows_ref, out_ref):
    place = place_of(position_ref, out_ref.shape[2])
    out_ref[...] = dot_nn(place, rows_ref[0]).astype(BF).reshape(out_ref.shape)


def route_kernel(first_ref, position_ref, rows_ref, mask_ref, router_ref, out_ref, slot_w_ref):
    _, count, capacity, width = out_ref.shape
    place = place_of(position_ref, capacity)
    rows = rows_ref[0]
    out_ref[...] = dot_nn(place, rows).astype(BF).reshape(out_ref.shape)
    chosen = jax.nn.sigmoid(dot_nn(rows, router_ref[...])) * mask_ref[0]
    weights = route_scale * chosen / jnp.sum(chosen, axis=1, keepdims=True)
    high = weights.astype(BF)
    low = (weights - high.astype(F32)).astype(BF)
    spread = dot_nn(place, high) + dot_nn(place, low)
    lane = lax.broadcasted_iota(jnp.int32, spread.shape, 1)
    slot_expert = lax.broadcasted_iota(jnp.int32, spread.shape, 0) // capacity + first_ref[0]
    mine = jnp.sum(jnp.where(lane == slot_expert, spread, 0.0), axis=1, keepdims=True)
    slot_w_ref[...] = jnp.broadcast_to(mine, spread.shape).reshape(slot_w_ref.shape)


def dispatch(position, rows, capacity):
    groups, count, tokens = position.shape
    width = rows.shape[1]
    return pl.pallas_call(
        dispatch_kernel,
        grid=(groups,),
        in_specs=[
            pl.BlockSpec((1, count, tokens), lambda s: (s, 0, 0)),
            pl.BlockSpec((1, tokens, width), lambda s: (s, 0, 0)),
        ],
        out_specs=pl.BlockSpec((1, count, capacity, width), lambda s: (s, 0, 0, 0)),
        out_shape=jax.ShapeDtypeStruct((groups, count, capacity, width), BF),
        name="dispatch",
    )(position, rows.reshape((groups, tokens, width)))


def dispatch_route(first, position, rows, mask, router, capacity):
    groups, count, tokens = position.shape
    width = rows.shape[1]
    lanes = router.shape[1]
    slab = lambda cols: pl.BlockSpec((1, count, capacity, cols), lambda s, _: (s, 0, 0, 0))
    return pl.pallas_call(
        route_kernel,
        grid_spec=pltpu.PrefetchScalarGridSpec(
            num_scalar_prefetch=1,
            grid=(groups,),
            in_specs=[
                pl.BlockSpec((1, count, tokens), lambda s, _: (s, 0, 0)),
                pl.BlockSpec((1, tokens, width), lambda s, _: (s, 0, 0)),
                pl.BlockSpec((1, tokens, lanes), lambda s, _: (s, 0, 0)),
                pl.BlockSpec((width, lanes), lambda s, _: (0, 0)),
            ],
            out_specs=[slab(width), slab(lanes)],
        ),
        out_shape=[
            jax.ShapeDtypeStruct((groups, count, capacity, width), BF),
            jax.ShapeDtypeStruct((groups, count, capacity, lanes), F32),
        ],
        name="dispatch_route",
    )(first, position, rows.reshape((groups, tokens, width)), mask, router)


def expert_kernel(
    first_ref, rows_ref, grads_ref, weights_ref, slot_w_ref,
    out_a_ref, out_b_ref, back_a_ref, back_b_ref, saved_ref,
):
    groups, _, capacity, width = rows_ref.shape
    slots = groups * capacity
    rows = rows_ref[...].reshape((slots, width))
    grads = grads_ref[...].reshape((slots, width))
    gate = matmul_t(rows, weights_ref[0, 0])
    up = matmul_t(rows, weights_ref[0, 1])
    d_plain = matmul_t(grads, weights_ref[0, 2])
    slot_w = slot_w_ref[...].reshape((slots, slot_w_ref.shape[-1]))[:, :1]
    sigma = jax.nn.sigmoid(gate)
    silu = gate * sigma
    hidden = silu * up
    d_weight = jnp.sum(hidden * d_plain, axis=1, keepdims=True)
    hidden_w = (hidden * slot_w).astype(BF)
    d_hidden = d_plain * slot_w
    d_gate = (d_hidden * up * sigma * (1.0 + gate * (1.0 - sigma))).astype(BF)
    d_up = (d_hidden * silu).astype(BF)
    saved_ref[0, 0] = d_gate
    saved_ref[0, 1] = d_up
    saved_ref[0, 2] = hidden_w
    half = out_a_ref.shape[-1]
    shape_half = (groups, 1, capacity, half)
    for part, out_ref, back_ref in ((0, out_a_ref, back_a_ref), (1, out_b_ref, back_b_ref)):
        cols = pl.ds(part * half, half)
        back = dot_nn(d_gate, weights_ref[0, 0, :, cols]) + dot_nn(
            d_up, weights_ref[0, 1, :, cols]
        )
        back_ref[:, :, :, :half] = back.astype(BF).reshape(shape_half)
        out_ref[...] = dot_nn(hidden_w, weights_ref[0, 2, :, cols]).astype(BF).reshape(shape_half)
    spare = back_b_ref.shape[-1] - half
    lane = lax.broadcasted_iota(jnp.int32, (slots, spare), 1)
    spread = jnp.where(lane == first_ref[0] + pl.program_id(0), d_weight, 0.0)
    back_b_ref[:, :, :, half:] = spread.astype(BF).reshape((groups, 1, capacity, spare))


def group_tile(groups, capacity):
    return max(t for t in range(1, groups + 1) if groups % t == 0 and t * capacity <= 512)


def expert_math(first, rows, grads, experts_t, slot_w, spare):
    groups, count, capacity, width = rows.shape
    hidden = experts_t.shape[2]
    tile = group_tile(groups, capacity)
    half = width // 2
    slab = lambda cols: pl.BlockSpec((tile, 1, capacity, cols), lambda e, s, _: (s, e, 0, 0))
    shape = lambda cols: jax.ShapeDtypeStruct((groups, count, capacity, cols), BF)
    slots = groups * capacity
    return pl.pallas_call(
        expert_kernel,
        grid_spec=pltpu.PrefetchScalarGridSpec(
            num_scalar_prefetch=1,
            grid=(count, groups // tile),
            in_specs=[
                slab(width),
                slab(width),
                pl.BlockSpec((1, 3, hidden, width), lambda e, s, _: (e, 0, 0, 0)),
                slab(slot_w.shape[-1]),
            ],
            out_specs=[
                slab(half),
                slab(half),
                slab(half),
                slab(half + spare),
                pl.BlockSpec((1, 3, tile * capacity, hidden), lambda e, s, _: (e, 0, s, 0)),
            ],
        ),
        out_shape=[
            shape(half),
            shape(half),
            shape(half),
            shape(half + spare),
            jax.ShapeDtypeStruct((count, 3, slots, hidden), BF),
        ],
        compiler_params=pltpu.CompilerParams(vmem_limit_bytes=60 * 1024 * 1024),
        name="expert_math",
    )(first, rows, grads, experts_t, slot_w)


def expert_grad_kernel(rows_ref, grads_ref, saved_ref, out_ref):
    groups, _, capacity, width = rows_ref.shape
    slots = groups * capacity
    rows = rows_ref[...].reshape((slots, width))
    grads = grads_ref[...].reshape((slots, width))
    found = (
        matmul_tl(saved_ref[0, 0], rows),
        matmul_tl(saved_ref[0, 1], rows),
        matmul_tl(saved_ref[0, 2], grads),
    )

    @pl.when(pl.program_id(1) == 0)
    def _():
        for which in range(3):
            out_ref[0, which] = found[which]

    @pl.when(pl.program_id(1) > 0)
    def _():
        for which in range(3):
            out_ref[0, which] += found[which]


def expert_grads(rows, grads, saved):
    groups, count, capacity, width = rows.shape
    hidden = saved.shape[3]
    tile = group_tile(groups, capacity)
    slab = pl.BlockSpec((tile, 1, capacity, width), lambda e, s: (s, e, 0, 0))
    return pl.pallas_call(
        expert_grad_kernel,
        grid=(count, groups // tile),
        in_specs=[
            slab,
            slab,
            pl.BlockSpec((1, 3, tile * capacity, hidden), lambda e, s: (e, 0, s, 0)),
        ],
        out_specs=pl.BlockSpec((1, 3, hidden, width), lambda e, s: (e, 0, 0, 0)),
        out_shape=jax.ShapeDtypeStruct((count, 3, hidden, width), F32),
        compiler_params=pltpu.CompilerParams(vmem_limit_bytes=60 * 1024 * 1024),
        name="expert_grads",
    )(rows, grads, saved)


def combine_kernel(core_ref, position_ref, values_ref, keep_ref, send_ref):
    _, count, capacity, width = values_ref.shape
    tokens = position_ref.shape[2]
    own = tokens // (2 * keep_ref.shape[1])
    place = place_of(position_ref, capacity)
    found = matmul_tl(place, values_ref[...].reshape((count * capacity, width))).astype(BF)
    found = found.reshape((keep_ref.shape[1], 2, own, width))
    for core in range(2):

        @pl.when(core_ref[0] == core)
        def _():
            keep_ref[0] = found[:, core]
            send_ref[0] = found[:, 1 - core]


def combine(position, values, order):
    groups, count, tokens = position.shape
    capacity, width = values.shape[2:]
    size = lax.axis_size("tensor")
    outer, inner = factors("tensor")
    own = tokens // size
    far_dp, near_dp = factors("dp")
    core = lax.axis_index("tensor") % inner
    slab = pl.BlockSpec((1, outer, own, width), lambda s, _: (s, 0, 0, 0))
    shape = jax.ShapeDtypeStruct((groups, outer, own, width), BF)
    keep, send = pl.pallas_call(
        combine_kernel,
        grid_spec=pltpu.PrefetchScalarGridSpec(
            num_scalar_prefetch=1,
            grid=(groups,),
            in_specs=[
                pl.BlockSpec((1, count, tokens), lambda s, _: (s, 0, 0)),
                pl.BlockSpec((1, count, capacity, width), lambda s, _: (s, 0, 0, 0)),
            ],
            out_specs=[slab, slab],
        ),
        out_shape=[shape, shape],
        name="combine",
    )(core.reshape((1,)).astype(jnp.int32), position, values)
    other = lax.ppermute(send, "tensor", factor_pairs(size, 1, inner, 1))
    total = (keep.astype(F32) + other.astype(F32)).astype(BF)
    total = total.reshape((far_dp, near_dp, outer, own, width))
    if order == "tensor first":
        total = scatter_factor(total, 2, "tensor", inner, outer)
        total = scatter_factor(total, 1, "dp", 1, near_dp)
    else:
        total = scatter_factor(total, 1, "dp", 1, near_dp)
        total = scatter_factor(total, 1, "tensor", inner, outer)
    return scatter_factor(total, 0, "dp", near_dp, far_dp, True)


def split_high_low(values):
    high = values.astype(BF)
    return high, (values - high.astype(F32)).astype(BF)


def body(
    tokens,
    segments,
    expert_ids,
    cotangent,
    attn_gain,
    ffn_gain,
    latent_gain,
    latent_down,
    router_proj,
    query_proj,
    kv_expand,
    output_proj,
    shared_gate,
    shared_up,
    shared_down,
    experts,
):
    both = ("dp", "tensor")
    n_dp, n_tensor = lax.axis_size("dp"), lax.axis_size("tensor")
    n_all = n_dp * n_tensor
    dp_index, tensor_index = lax.axis_index("dp"), lax.axis_index("tensor")
    own_rows, model_width = tokens.shape
    count = own_rows * n_tensor
    first_row = tensor_index * own_rows
    down_rows, lat_rope = latent_down.shape
    local_experts = experts.shape[0]
    capacity = count * TOPK * 4 // (3 * EXPERTS)
    slots = local_experts * capacity
    doc_ids = segments[0]

    small_width = lat_rope + EXPERTS
    own_ids = lax.dynamic_slice_in_dim(expert_ids, first_row, own_rows, 0)
    gain_piece, lat_piece = attn_gain.shape[0], latent_gain.shape[0]
    gain_row = jnp.concatenate([attn_gain, ffn_gain, latent_gain])
    gain_row = jnp.pad(gain_row, (0, small_width - gain_row.shape[0]))[None]
    id_rows = -(-own_rows * TOPK // small_width)
    ids_flat = own_ids.astype(BF).reshape(-1)
    ids_flat = jnp.pad(ids_flat, (0, id_rows * small_width - ids_flat.shape[0]))
    extra_rows = -(-(1 + id_rows) // 16) * 16
    small = jnp.concatenate(
        [
            jnp.concatenate([latent_down, router_proj], axis=1),
            gain_row,
            ids_flat.reshape((id_rows, small_width)),
            jnp.zeros((extra_rows - 1 - id_rows, small_width), BF),
        ],
        axis=0,
    )
    small_four = lax.all_gather(small, "tensor", axis=0, tiled=True)
    tokens_in, _ = lax.optimization_barrier((tokens, small_four))
    rows_all = lax.all_gather(tokens_in, "tensor", axis=0, tiled=True)
    small_all = gather_rows(small_four, "dp").reshape(
        (n_all, down_rows + extra_rows, small_width)
    )
    query_full = gather_rows(query_proj, "dp")
    expand_full = gather_rows(kv_expand, "dp")
    out_full = gather_rows(output_proj, "dp")
    cot_in, _ = lax.optimization_barrier((cotangent, rows_all))
    cot_all = lax.all_gather(cot_in, both, axis=0, tiled=True)
    sff = shared_gate.shape[1]
    shared_mine = jnp.concatenate(
        [jnp.transpose(shared_gate), jnp.transpose(shared_up), jnp.transpose(shared_down)], axis=0
    )
    shared_mine, _ = lax.optimization_barrier((shared_mine, out_full))
    shared_full = gather_columns(shared_mine, "dp")
    sgate_full = shared_full[:sff]
    sup_full = shared_full[sff : 2 * sff]
    sdown_full = shared_full[2 * sff :]

    down_router = small_all[:, :down_rows].reshape((n_all * down_rows, small_width))
    down_full = down_router[:, :lat_rope]
    router_full = down_router[:, lat_rope:]
    gains = small_all[:, down_rows].astype(F32)
    gain_one = gains[:, :gain_piece].reshape(-1)
    gain_two = gains[:, gain_piece : 2 * gain_piece].reshape(-1)
    gain_lat = gains[:, 2 * gain_piece : 2 * gain_piece + lat_piece].reshape(-1)
    ids_all = (
        small_all[:, down_rows + 1 : down_rows + 1 + id_rows]
        .reshape((n_all, id_rows * small_width))[:, : own_rows * TOPK]
        .astype(jnp.int32)
        .reshape((n_dp, count, TOPK))
    )

    first_expert = dp_index * local_experts
    here = first_expert + jnp.arange(local_experts, dtype=jnp.int32)
    named = jnp.any(ids_all[:, None, :, :] == here[None, :, None, None], axis=-1)
    token_pos = jnp.arange(count, dtype=jnp.int32)
    earlier = (token_pos[:, None] < token_pos[None, :]).astype(BF)
    position = lax.dot_general(
        named.astype(BF).reshape((n_dp * local_experts, count)),
        earlier,
        (((1,), (0,)), ((), ())),
        preferred_element_type=F32,
    ).reshape((n_dp, local_experts, count))
    position = jnp.where(named, position, -1.0)
    every = jnp.arange(EXPERTS, dtype=jnp.int32)
    spare = -(-EXPERTS // 128) * 128
    chosen_mask = jnp.any(ids_all[:, :, :, None] == every[None, None, None, :], axis=2).astype(F32)
    mask_wide = jnp.pad(chosen_mask, ((0, 0), (0, 0), (0, spare - EXPERTS)))
    router_wide = jnp.pad(router_full, ((0, 0), (0, spare - EXPERTS)))

    width_q = NOPE + ROPE
    local_heads = query_full.shape[1] // width_q
    cosines, sines = rope_tables(count, ROPE)
    residual = rows_all.astype(F32)
    inv_one = rms_scale(residual)
    normed_one = (residual * inv_one * gain_one).astype(BF)
    latent = jnp.dot(normed_one, down_full, preferred_element_type=F32)
    query = jnp.dot(normed_one, query_full, preferred_element_type=F32).reshape(
        (count, local_heads, width_q)
    )
    compressed = latent[:, :LAT]
    inv_lat = rms_scale(compressed)
    comp_normed = (compressed * inv_lat * gain_lat).astype(BF)
    expanded = jnp.dot(comp_normed, expand_full, preferred_element_type=F32).reshape(
        (count, local_heads, NOPE + VDIM)
    )
    query_rot = rotate(query[:, :, NOPE:], cosines[:, None, :], sines[:, None, :])
    key_rot = rotate(latent[:, LAT:], cosines, sines)
    query_all = jnp.concatenate([query[:, :, :NOPE], query_rot], axis=-1).astype(BF)
    key_all = jnp.concatenate(
        [expanded[:, :, :NOPE], jnp.broadcast_to(key_rot[:, None, :], (count, local_heads, ROPE))],
        axis=-1,
    ).astype(BF)
    value_all = expanded[:, :, NOPE:].astype(BF)
    context, log_total = attend(query_all, key_all, value_all, doc_ids)
    context_b = context.reshape((count, local_heads * VDIM)).astype(BF)
    attn_own = scatter_rows(matmul_t(context_b, out_full), "tensor")
    middle = tokens.astype(F32) + attn_own
    inv_two = rms_scale(middle)
    normed_two_own = (middle * inv_two * gain_two).astype(BF)
    normed_all = lax.all_gather(normed_two_own, both, axis=0, tiled=True)

    experts_t = jnp.swapaxes(experts, 2, 3)
    first = first_expert.reshape((1,)).astype(jnp.int32)
    grads_disp = dispatch(position, cot_all, capacity)
    rows_disp, slot_w = dispatch_route(
        first, position, normed_all, mask_wide, router_wide, capacity
    )
    out_a, out_b, back_a, back_b, saved = expert_math(
        first, rows_disp, grads_disp, experts_t, slot_w, spare
    )
    half = model_width // 2
    back_own_a = combine(position, back_a, "tensor first")
    back_own_b = combine(position, back_b, "dp first")
    grad_experts = jnp.swapaxes(expert_grads(rows_disp, grads_disp, saved), 2, 3)
    out_own_a = combine(position, out_a, "tensor first")
    out_own_b = combine(position, out_b, "dp first")

    seq_row = dp_index * count
    normed_two = lax.dynamic_slice_in_dim(normed_all, seq_row, count, 0)
    grad_all = lax.dynamic_slice_in_dim(cot_all, seq_row, count, 0)
    shared_pre_gate = matmul_t(normed_two, sgate_full)
    shared_pre_up = matmul_t(normed_two, sup_full)
    sigma_shared = jax.nn.sigmoid(shared_pre_gate)
    shared_hidden = (shared_pre_gate * sigma_shared * shared_pre_up).astype(BF)
    d_shared = matmul_t(grad_all, sdown_full)
    d_sgate = (
        d_shared * shared_pre_up * sigma_shared * (1.0 + shared_pre_gate * (1.0 - sigma_shared))
    ).astype(BF)
    d_sup = (d_shared * shared_pre_gate * sigma_shared).astype(BF)
    d_shared_own = scatter_rows(dot_nn(d_sgate, sgate_full) + dot_nn(d_sup, sup_full), "tensor")
    shared_own = scatter_rows(dot_nn(shared_hidden, sdown_full), "tensor")
    shared_grads = scatter_products(
        [d_sgate, d_sup, shared_hidden], [normed_two, normed_two, grad_all], "dp"
    )
    block_out = middle + shared_own + jnp.concatenate([out_own_a, out_own_b], axis=1)

    own_first = seq_row + first_row
    d_weight = back_own_b[:, half : half + EXPERTS]
    mask_own = lax.dynamic_slice_in_dim(
        chosen_mask.reshape((n_dp * count, EXPERTS)), own_first, own_rows, 0
    )
    scores_own = jax.nn.sigmoid(dot_nn(normed_two_own, router_full))
    chosen_own = scores_own * mask_own
    total_own = jnp.sum(chosen_own, axis=1, keepdims=True)
    d_chosen = route_scale * (
        d_weight / total_own
        - jnp.sum(d_weight * chosen_own, axis=1, keepdims=True) / (total_own * total_own)
    )
    d_logits = (d_chosen * mask_own * scores_own * (1.0 - scores_own)).astype(BF)
    d_normed_two = (
        d_shared_own
        + jnp.concatenate([back_own_a, back_own_b[:, :half]], axis=1)
        + matmul_t(d_logits, router_full)
    )
    grad_gain_two = jnp.sum(d_normed_two * middle * inv_two, axis=0)
    d_middle = cotangent.astype(F32) + norm_back(d_normed_two, middle, inv_two, gain_two)
    two_high, two_low = split_high_low(grad_gain_two)
    mid_sent = jnp.concatenate(
        [
            jnp.concatenate(
                [d_middle.astype(BF), jnp.pad(d_logits, ((0, 0), (0, spare - EXPERTS)))], axis=1
            ),
            jnp.pad(jnp.stack([two_high, two_low]), ((0, 14), (0, spare))),
        ],
        axis=0,
    )
    mid_all = gather_rows(mid_sent, "tensor").reshape(
        (n_tensor, own_rows + 16, model_width + spare)
    )
    d_mid_b = mid_all[:, :own_rows, :model_width].reshape((count, model_width))
    d_logits_seq = mid_all[:, :own_rows, model_width : model_width + EXPERTS].reshape(
        (count, EXPERTS)
    )
    gain_two_sum = jnp.sum(mid_all[:, own_rows : own_rows + 2, :model_width].astype(F32), axis=(0, 1))
    grad_out = scatter_rows(matmul_tl(d_mid_b, context_b), "dp")
    d_context = (
        jnp.dot(d_mid_b, out_full, preferred_element_type=F32)
        .astype(BF)
        .reshape((count, local_heads, VDIM))
    )
    d_query, d_key, d_value = attend_back(
        query_all, key_all, value_all, doc_ids, log_total, d_context
    )
    d_query_rot = unrotate(d_query[:, :, NOPE:], cosines[:, None, :], sines[:, None, :])
    d_query_all = (
        jnp.concatenate([d_query[:, :, :NOPE], d_query_rot], axis=-1)
        .reshape((count, local_heads * width_q))
        .astype(BF)
    )
    d_expanded = (
        jnp.concatenate([d_key[:, :, :NOPE], d_value], axis=-1)
        .reshape((count, local_heads * (NOPE + VDIM)))
        .astype(BF)
    )
    d_key_rot = jnp.sum(d_key[:, :, NOPE:], axis=1)
    back_own = scatter_rows(
        jnp.concatenate(
            [
                matmul_t(d_query_all, query_full).astype(BF),
                matmul_t(d_expanded, expand_full).astype(BF),
                d_key_rot.astype(BF),
                jnp.zeros((count, ROPE), BF),
            ],
            axis=1,
        ),
        "tensor",
    )
    grad_query = scatter_rows(matmul_tl(normed_one, d_query_all), "dp")
    grad_expand = scatter_rows(matmul_tl(comp_normed, d_expanded), "dp")
    d_rows_query = back_own[:, :model_width]
    d_comp_own = back_own[:, model_width : model_width + LAT]
    d_rot_own = back_own[:, model_width + LAT : model_width + LAT + ROPE]
    seq_own = lambda values: lax.dynamic_slice_in_dim(values, first_row, own_rows, 0)
    compressed_own, inv_lat_own = seq_own(compressed), seq_own(inv_lat)
    grad_gain_lat = jnp.sum(d_comp_own * compressed_own * inv_lat_own, axis=0)
    d_comp = norm_back(d_comp_own, compressed_own, inv_lat_own, gain_lat)
    d_latent = jnp.concatenate(
        [d_comp, unrotate(d_rot_own, seq_own(cosines), seq_own(sines))], axis=-1
    ).astype(BF)
    lat_high, lat_low = split_high_low(grad_gain_lat)
    lat_sent = jnp.concatenate(
        [d_latent, jnp.pad(jnp.stack([lat_high, lat_low]), ((0, 14), (0, lat_rope - LAT)))], axis=0
    )
    lat_all = gather_rows(lat_sent, "tensor").reshape(
        (n_tensor, own_rows + 16, lat_rope)
    )
    d_latent_seq = lat_all[:, :own_rows].reshape((count, lat_rope))
    gain_lat_sum = jnp.sum(lat_all[:, own_rows : own_rows + 2, :LAT].astype(F32), axis=(0, 1))
    residual_own, inv_one_own = tokens.astype(F32), seq_own(inv_one)
    d_normed_one = d_rows_query + matmul_t(d_latent, down_full)
    grad_gain_one = jnp.sum(d_normed_one * residual_own * inv_one_own, axis=0)
    grad_tokens = d_middle + norm_back(d_normed_one, residual_own, inv_one_own, gain_one)
    gain_one_share = scatter_rows(
        jnp.swapaxes(grad_gain_one.reshape((n_dp, n_tensor, gain_piece)), 0, 1), "tensor"
    )[0]

    def own_share(values, piece):
        view = values.reshape((n_dp, n_tensor, piece) + values.shape[1:])
        return pick(view, tensor_index, 1)

    wide = jnp.concatenate(
        [
            own_share(matmul_tl(normed_one, d_latent_seq), down_rows),
            own_share(matmul_tl(normed_two, d_logits_seq), down_rows),
        ],
        axis=2,
    )
    gain_line = jnp.concatenate(
        [gain_one_share, own_share(gain_two_sum, gain_piece), own_share(gain_lat_sum, lat_piece)],
        axis=1,
    )
    gain_line = jnp.pad(
        gain_line[:, None, :], ((0, 0), (0, 15), (0, small_width - 2 * gain_piece - lat_piece))
    )
    small_sum = scatter_rows(
        jnp.concatenate([wide, gain_line], axis=1).reshape((n_dp * (down_rows + 16), small_width)),
        "dp",
    )
    gain_out = small_sum[down_rows]
    return (
        block_out,
        grad_tokens,
        gain_out[:gain_piece],
        gain_out[gain_piece : 2 * gain_piece],
        gain_out[2 * gain_piece : 2 * gain_piece + lat_piece],
        small_sum[:down_rows, :lat_rope],
        small_sum[:down_rows, lat_rope:],
        grad_query,
        grad_expand,
        grad_out,
        jnp.transpose(shared_grads[:sff]),
        jnp.transpose(shared_grads[sff : 2 * sff]),
        jnp.transpose(shared_grads[2 * sff :]),
        grad_experts,
    )


def solution(mesh):
    in_specs = (
        P(("dp", "tensor"), None),
        P("dp", None),
        P("dp", None),
        P(("dp", "tensor"), None),
        P(("dp", "tensor")),
        P(("dp", "tensor")),
        P(("dp", "tensor")),
        P(("dp", "tensor"), None),
        P(("dp", "tensor"), None),
        P("dp", "tensor"),
        P("dp", "tensor"),
        P("dp", "tensor"),
        P("dp", "tensor"),
        P("dp", "tensor"),
        P("dp", "tensor"),
        P("dp", None, None, "tensor"),
    )
    out_specs = (
        P(("dp", "tensor"), None),
        P(("dp", "tensor"), None),
        P(("dp", "tensor")),
        P(("dp", "tensor")),
        P(("dp", "tensor")),
        P(("dp", "tensor"), None),
        P(("dp", "tensor"), None),
        P("dp", "tensor"),
        P("dp", "tensor"),
        P("dp", "tensor"),
        P("dp", "tensor"),
        P("dp", "tensor"),
        P("dp", "tensor"),
        P("dp", None, None, "tensor"),
    )
    return jax.shard_map(body, mesh=mesh, in_specs=in_specs, out_specs=out_specs, check_vma=False)
```

```python
import math

import jax
import jax.numpy as jnp
from jax import lax
from jax.experimental import pallas as pl
from jax.experimental.pallas import tpu as pltpu
from jax.experimental.layout import Layout, with_layout_constraint
from jax.sharding import PartitionSpec as P

NOPE = 128
ROPE = 64
VDIM = 128
LAT = 512
EXPERTS = 64
TOPK = 6


eps = 1e-06
route_scale = 2.446
rope_base = 50000.0


def rms_scale(values):
    return lax.rsqrt(jnp.mean(values * values, axis=-1, keepdims=True) + eps)


def norm_back(grad_normed, values, inverse, gain):
    scaled = grad_normed * gain
    return inverse * scaled - values * inverse * inverse * inverse * jnp.mean(
        scaled * values, axis=-1, keepdims=True
    )


def rope_tables(count, width):
    half = width // 2
    powers = jnp.arange(half, dtype=jnp.int32).astype(jnp.float32) * (2.0 / width)
    freqs = jnp.exp(-math.log(rope_base) * powers)
    angles = jnp.arange(count, dtype=jnp.int32).astype(jnp.float32)[:, None] * freqs[None, :]
    return (jnp.cos(angles), jnp.sin(angles))


def rotate(values, cosines, sines):
    half = values.shape[-1] // 2
    first = values[..., :half]
    second = values[..., half:]
    return jnp.concatenate(
        [first * cosines - second * sines, second * cosines + first * sines], axis=-1
    )


def unrotate(grads, cosines, sines):
    half = grads.shape[-1] // 2
    first = grads[..., :half]
    second = grads[..., half:]
    return jnp.concatenate(
        [first * cosines + second * sines, second * cosines - first * sines], axis=-1
    )


def matmul_t(left, right):
    return lax.dot_general(
        left, right, (((1,), (1,)), ((), ())), preferred_element_type=jnp.float32
    )


def matmul_tl(left, right):
    return lax.dot_general(
        left, right, (((0,), (0,)), ((), ())), preferred_element_type=jnp.float32
    )


def attend(query_all, key_all, value_all, doc_ids):
    count = query_all.shape[0]
    block = min(512, count)
    scale = 1.0 / math.sqrt(query_all.shape[-1])
    key_pos = jnp.arange(count, dtype=jnp.int32)

    def one_block(begin):
        query_pos = begin + jnp.arange(block, dtype=jnp.int32)
        allowed = (doc_ids[:, None] == doc_ids[None, :]) & (key_pos[None, :] <= query_pos[:, None])
        scores = (
            jnp.einsum("qhc,khc->hqk", query_all, key_all, preferred_element_type=jnp.float32)
            * scale
        )
        raw_weights = jnp.where(allowed[None], jnp.exp(scores), 0.0)
        total = jnp.sum(raw_weights, axis=-1)
        probs = (raw_weights / total[..., None]).astype(jnp.bfloat16)
        context = jnp.einsum("hqk,khc->qhc", probs, value_all, preferred_element_type=jnp.float32)
        return (context, jnp.log(total))

    begins = jnp.arange(0, count, block, dtype=jnp.int32)
    contexts, logs = lax.map(one_block, begins)
    heads = query_all.shape[1]
    context = contexts.reshape((count, heads, value_all.shape[2]))
    log_total = jnp.transpose(logs, (1, 0, 2)).reshape((heads, count))
    return (context, log_total)


def attend_back(query_all, key_all, value_all, doc_ids, log_total, d_context):
    count = query_all.shape[0]
    heads = query_all.shape[1]
    block = min(512, count)
    scale = 1.0 / math.sqrt(query_all.shape[-1])
    key_pos = jnp.arange(count, dtype=jnp.int32)

    def one_block(carry, begin):
        d_keys, d_values = carry
        query_pos = begin + jnp.arange(block, dtype=jnp.int32)
        allowed = (doc_ids[:, None] == doc_ids[None, :]) & (key_pos[None, :] <= query_pos[:, None])
        scores = (
            jnp.einsum("qhc,khc->hqk", query_all, key_all, preferred_element_type=jnp.float32)
            * scale
        )
        probs = jnp.where(allowed[None], jnp.exp(scores - log_total[..., None]), 0.0)
        d_values = d_values + jnp.einsum(
            "hqk,qhc->khc",
            probs.astype(jnp.bfloat16),
            d_context,
            preferred_element_type=jnp.float32,
        )
        d_probs = jnp.einsum(
            "qhc,khc->hqk", d_context, value_all, preferred_element_type=jnp.float32
        )
        delta = jnp.sum(probs * d_probs, axis=-1, keepdims=True)
        d_scores = (probs * (d_probs - delta) * scale).astype(jnp.bfloat16)
        d_queries = jnp.einsum(
            "hqk,khc->qhc", d_scores, key_all, preferred_element_type=jnp.float32
        )
        d_keys = d_keys + jnp.einsum(
            "hqk,qhc->khc", d_scores, query_all, preferred_element_type=jnp.float32
        )
        return ((d_keys, d_values), d_queries)

    begins = jnp.arange(0, count, block, dtype=jnp.int32)
    start_state = (jnp.zeros(key_all.shape, jnp.float32), jnp.zeros(value_all.shape, jnp.float32))
    (d_keys, d_values), d_queries = lax.scan(one_block, start_state, begins)
    return (d_queries.reshape((count, heads, query_all.shape[2])), d_keys, d_values)


BF = jnp.bfloat16
F32 = jnp.float32


def row_major(array):
    return with_layout_constraint(array, Layout(major_to_minor=tuple(range(array.ndim))))


def factor_pairs(size, stride, parts, shift):
    pairs = []
    for index in range(size):
        place = index // stride % parts
        pairs.append((index, index + ((place + shift) % parts - place) * stride))
    return pairs


def pick(array, index, dim):
    return lax.dynamic_index_in_dim(array, index, dim, keepdims=False)


def scatter_factor(array, dim, axis, stride, parts, final=False):
    size = lax.axis_size(axis)
    place = lax.axis_index(axis) // stride % parts
    received = [
        lax.ppermute(
            pick(array, (place + shift) % parts, dim),
            axis,
            factor_pairs(size, stride, parts, shift),
        )
        for shift in range(1, parts)
    ]
    total = pick(array, place, dim).astype(F32)
    for item in received:
        total = total + item.astype(F32)
    return total if final else total.astype(BF)


def factors(axis):
    size = lax.axis_size(axis)
    inner = 2 if size % 2 == 0 else 1
    return size // inner, inner


def gather_pieces(shard, axis):
    size = lax.axis_size(axis)
    outer, inner = factors(axis)
    index = lax.axis_index(axis)
    far, near = index // inner, index % inner
    pieces = [shard] + [
        lax.ppermute(shard, axis, factor_pairs(size, inner, outer, shift))
        for shift in range(1, outer)
    ]
    found = []
    for shift, piece in enumerate(pieces):
        source = (far - shift) % outer
        found.append((source, near, piece))
        for turn in range(1, inner):
            other = lax.ppermute(piece, axis, factor_pairs(size, 1, inner, turn))
            found.append((source, (near - turn) % inner, other))
    return found


def gather_rows(shard, axis):
    inner = factors(axis)[1]
    rows = shard.shape[0]
    full = jnp.zeros((lax.axis_size(axis) * rows,) + shard.shape[1:], shard.dtype)
    rest = (0,) * (shard.ndim - 1)
    for far, near, piece in gather_pieces(shard, axis):
        full = lax.dynamic_update_slice(full, piece, ((far * inner + near) * rows,) + rest)
    return full


def gather_columns(shard, axis):
    inner = factors(axis)[1]
    rows, columns = shard.shape
    full = jnp.zeros((rows, lax.axis_size(axis) * columns), shard.dtype)
    for far, near, piece in gather_pieces(shard, axis):
        full = lax.dynamic_update_slice(full, piece, (0, (far * inner + near) * columns))
    return full


def scatter_rows(array, axis, final=True):
    outer, inner = factors(axis)
    rows = array.shape[0] // (outer * inner)
    view = row_major(array.astype(BF)).reshape((outer, inner, rows) + array.shape[1:])
    view = scatter_factor(view, 1, axis, 1, inner)
    return scatter_factor(view, 0, axis, inner, outer, final)


def scatter_products(lefts, rights, axis):
    size = lax.axis_size(axis)
    outer, inner = factors(axis)
    near = lax.axis_index(axis) % inner
    columns = rights[0].shape[1] // size

    def blocks(which):
        made = []
        for far in range(outer):
            begin = (far * inner + which) * columns
            made.append(
                jnp.concatenate(
                    [
                        matmul_tl(left, lax.dynamic_slice_in_dim(right, begin, columns, 1)).astype(BF)
                        for left, right in zip(lefts, rights)
                    ],
                    axis=0,
                )
            )
        return jnp.stack(made)

    sent = [
        lax.ppermute(blocks((near + turn) % inner), axis, factor_pairs(size, 1, inner, turn))
        for turn in range(1, inner)
    ]
    total = blocks(near)
    if sent:
        total = total.astype(F32)
        for item in sent:
            total = total + item.astype(F32)
        total = total.astype(BF)
    return scatter_factor(total, 0, axis, inner, outer, True)


def dot_nn(left, right):
    return lax.dot_general(left, right, (((1,), (0,)), ((), ())), preferred_element_type=F32)


def place_of(position_ref, capacity):
    _, count, tokens = position_ref.shape
    slot = lax.broadcasted_iota(jnp.int32, (capacity, tokens), 0).astype(F32)
    return jnp.concatenate(
        [
            jnp.where(position_ref[0, e : e + 1, :] == slot, 1.0, 0.0).astype(BF)
            for e in range(count)
        ],
        axis=0,
    )


def dispatch_kernel(position_ref, rows_ref, out_ref):
    place = place_of(position_ref, out_ref.shape[2])
    out_ref[...] = dot_nn(place, rows_ref[0]).astype(BF).reshape(out_ref.shape)


def route_kernel(first_ref, position_ref, rows_ref, mask_ref, router_ref, out_ref, slot_w_ref):
    _, count, capacity, width = out_ref.shape
    place = place_of(position_ref, capacity)
    rows = rows_ref[0]
    out_ref[...] = dot_nn(place, rows).astype(BF).reshape(out_ref.shape)
    chosen = jax.nn.sigmoid(dot_nn(rows, router_ref[...])) * mask_ref[0]
    weights = route_scale * chosen / jnp.sum(chosen, axis=1, keepdims=True)
    high = weights.astype(BF)
    low = (weights - high.astype(F32)).astype(BF)
    spread = dot_nn(place, high) + dot_nn(place, low)
    lane = lax.broadcasted_iota(jnp.int32, spread.shape, 1)
    slot_expert = lax.broadcasted_iota(jnp.int32, spread.shape, 0) // capacity + first_ref[0]
    mine = jnp.sum(jnp.where(lane == slot_expert, spread, 0.0), axis=1, keepdims=True)
    slot_w_ref[...] = jnp.broadcast_to(mine, spread.shape).reshape(slot_w_ref.shape)


def dispatch(position, rows, capacity):
    groups, count, tokens = position.shape
    width = rows.shape[1]
    return pl.pallas_call(
        dispatch_kernel,
        grid=(groups,),
        in_specs=[
            pl.BlockSpec((1, count, tokens), lambda s: (s, 0, 0)),
            pl.BlockSpec((1, tokens, width), lambda s: (s, 0, 0)),
        ],
        out_specs=pl.BlockSpec((1, count, capacity, width), lambda s: (s, 0, 0, 0)),
        out_shape=jax.ShapeDtypeStruct((groups, count, capacity, width), BF),
        name="dispatch",
    )(position, rows.reshape((groups, tokens, width)))


def dispatch_route(first, position, rows, mask, router, capacity):
    groups, count, tokens = position.shape
    width = rows.shape[1]
    lanes = router.shape[1]
    slab = lambda cols: pl.BlockSpec((1, count, capacity, cols), lambda s, _: (s, 0, 0, 0))
    return pl.pallas_call(
        route_kernel,
        grid_spec=pltpu.PrefetchScalarGridSpec(
            num_scalar_prefetch=1,
            grid=(groups,),
            in_specs=[
                pl.BlockSpec((1, count, tokens), lambda s, _: (s, 0, 0)),
                pl.BlockSpec((1, tokens, width), lambda s, _: (s, 0, 0)),
                pl.BlockSpec((1, tokens, lanes), lambda s, _: (s, 0, 0)),
                pl.BlockSpec((width, lanes), lambda s, _: (0, 0)),
            ],
            out_specs=[slab(width), slab(lanes)],
        ),
        out_shape=[
            jax.ShapeDtypeStruct((groups, count, capacity, width), BF),
            jax.ShapeDtypeStruct((groups, count, capacity, lanes), F32),
        ],
        name="dispatch_route",
    )(first, position, rows.reshape((groups, tokens, width)), mask, router)


def expert_kernel(
    first_ref, rows_ref, grads_ref, weights_ref, slot_w_ref,
    out_a_ref, out_b_ref, back_a_ref, back_b_ref, saved_ref,
):
    groups, _, capacity, width = rows_ref.shape
    slots = groups * capacity
    rows = rows_ref[...].reshape((slots, width))
    grads = grads_ref[...].reshape((slots, width))
    gate = matmul_t(rows, weights_ref[0, 0])
    up = matmul_t(rows, weights_ref[0, 1])
    d_plain = matmul_t(grads, weights_ref[0, 2])
    slot_w = slot_w_ref[...].reshape((slots, slot_w_ref.shape[-1]))[:, :1]
    sigma = jax.nn.sigmoid(gate)
    silu = gate * sigma
    hidden = silu * up
    d_weight = jnp.sum(hidden * d_plain, axis=1, keepdims=True)
    hidden_w = (hidden * slot_w).astype(BF)
    d_hidden = d_plain * slot_w
    d_gate = (d_hidden * up * sigma * (1.0 + gate * (1.0 - sigma))).astype(BF)
    d_up = (d_hidden * silu).astype(BF)
    saved_ref[0, 0] = d_gate
    saved_ref[0, 1] = d_up
    saved_ref[0, 2] = hidden_w
    half = out_a_ref.shape[-1]
    shape_half = (groups, 1, capacity, half)
    for part, out_ref, back_ref in ((0, out_a_ref, back_a_ref), (1, out_b_ref, back_b_ref)):
        cols = pl.ds(part * half, half)
        back = dot_nn(d_gate, weights_ref[0, 0, :, cols]) + dot_nn(
            d_up, weights_ref[0, 1, :, cols]
        )
        back_ref[:, :, :, :half] = back.astype(BF).reshape(shape_half)
        out_ref[...] = dot_nn(hidden_w, weights_ref[0, 2, :, cols]).astype(BF).reshape(shape_half)
    spare = back_b_ref.shape[-1] - half
    lane = lax.broadcasted_iota(jnp.int32, (slots, spare), 1)
    spread = jnp.where(lane == first_ref[0] + pl.program_id(0), d_weight, 0.0)
    back_b_ref[:, :, :, half:] = spread.astype(BF).reshape((groups, 1, capacity, spare))


def group_tile(groups, capacity):
    return max(t for t in range(1, groups + 1) if groups % t == 0 and t * capacity <= 512)


def expert_math(first, rows, grads, experts_t, slot_w, spare):
    groups, count, capacity, width = rows.shape
    hidden = experts_t.shape[2]
    tile = group_tile(groups, capacity)
    half = width // 2
    slab = lambda cols: pl.BlockSpec((tile, 1, capacity, cols), lambda e, s, _: (s, e, 0, 0))
    shape = lambda cols: jax.ShapeDtypeStruct((groups, count, capacity, cols), BF)
    slots = groups * capacity
    return pl.pallas_call(
        expert_kernel,
        grid_spec=pltpu.PrefetchScalarGridSpec(
            num_scalar_prefetch=1,
            grid=(count, groups // tile),
            in_specs=[
                slab(width),
                slab(width),
                pl.BlockSpec((1, 3, hidden, width), lambda e, s, _: (e, 0, 0, 0)),
                slab(slot_w.shape[-1]),
            ],
            out_specs=[
                slab(half),
                slab(half),
                slab(half),
                slab(half + spare),
                pl.BlockSpec((1, 3, tile * capacity, hidden), lambda e, s, _: (e, 0, s, 0)),
            ],
        ),
        out_shape=[
            shape(half),
            shape(half),
            shape(half),
            shape(half + spare),
            jax.ShapeDtypeStruct((count, 3, slots, hidden), BF),
        ],
        compiler_params=pltpu.CompilerParams(vmem_limit_bytes=60 * 1024 * 1024),
        name="expert_math",
    )(first, rows, grads, experts_t, slot_w)


def expert_grad_kernel(rows_ref, grads_ref, saved_ref, out_ref):
    groups, _, capacity, width = rows_ref.shape
    slots = groups * capacity
    rows = rows_ref[...].reshape((slots, width))
    grads = grads_ref[...].reshape((slots, width))
    found = (
        matmul_tl(saved_ref[0, 0], rows),
        matmul_tl(saved_ref[0, 1], rows),
        matmul_tl(saved_ref[0, 2], grads),
    )

    @pl.when(pl.program_id(1) == 0)
    def _():
        for which in range(3):
            out_ref[0, which] = found[which]

    @pl.when(pl.program_id(1) > 0)
    def _():
        for which in range(3):
            out_ref[0, which] += found[which]


def expert_grads(rows, grads, saved):
    groups, count, capacity, width = rows.shape
    hidden = saved.shape[3]
    tile = group_tile(groups, capacity)
    slab = pl.BlockSpec((tile, 1, capacity, width), lambda e, s: (s, e, 0, 0))
    return pl.pallas_call(
        expert_grad_kernel,
        grid=(count, groups // tile),
        in_specs=[
            slab,
            slab,
            pl.BlockSpec((1, 3, tile * capacity, hidden), lambda e, s: (e, 0, s, 0)),
        ],
        out_specs=pl.BlockSpec((1, 3, hidden, width), lambda e, s: (e, 0, 0, 0)),
        out_shape=jax.ShapeDtypeStruct((count, 3, hidden, width), F32),
        compiler_params=pltpu.CompilerParams(vmem_limit_bytes=60 * 1024 * 1024),
        name="expert_grads",
    )(rows, grads, saved)


def combine_kernel(core_ref, position_ref, values_ref, keep_ref, send_ref):
    _, count, capacity, width = values_ref.shape
    tokens = position_ref.shape[2]
    own = tokens // (2 * keep_ref.shape[1])
    place = place_of(position_ref, capacity)
    found = matmul_tl(place, values_ref[...].reshape((count * capacity, width))).astype(BF)
    found = found.reshape((keep_ref.shape[1], 2, own, width))
    for core in range(2):

        @pl.when(core_ref[0] == core)
        def _():
            keep_ref[0] = found[:, core]
            send_ref[0] = found[:, 1 - core]


def core_stage(position, values):
    groups, count, tokens = position.shape
    capacity, width = values.shape[2:]
    size = lax.axis_size("tensor")
    outer, inner = factors("tensor")
    own = tokens // size
    core = lax.axis_index("tensor") % inner
    slab = pl.BlockSpec((1, outer, own, width), lambda s, _: (s, 0, 0, 0))
    shape = jax.ShapeDtypeStruct((groups, outer, own, width), BF)
    keep, send = pl.pallas_call(
        combine_kernel,
        grid_spec=pltpu.PrefetchScalarGridSpec(
            num_scalar_prefetch=1,
            grid=(groups,),
            in_specs=[
                pl.BlockSpec((1, count, tokens), lambda s, _: (s, 0, 0)),
                pl.BlockSpec((1, count, capacity, width), lambda s, _: (s, 0, 0, 0)),
            ],
            out_specs=[slab, slab],
        ),
        out_shape=[shape, shape],
        name="combine",
    )(core.reshape((1,)).astype(jnp.int32), position, values)
    return [keep, lax.ppermute(send, "tensor", factor_pairs(size, 1, inner, 1))]


def sum_split_kernel(count, place_ref, *refs):
    parts = refs[0].shape[1]
    for shift, out_ref in enumerate(refs[count:]):
        index = lax.rem(place_ref[0] + shift, parts)
        total = refs[0][0, index].astype(F32)
        for ref in refs[1:count]:
            total = total + ref[0, index].astype(F32)
        out_ref[0] = total.astype(BF)


def stage(arrays, lead, axis, stride, parts):
    width = arrays[0].shape[-1]
    size = lax.axis_size(axis)
    place = lax.axis_index(axis) // stride % parts
    rows = arrays[0].size // (lead * parts * width)
    views = [array.reshape((lead, parts, rows, width)) for array in arrays]
    tile = 32 if rows % 32 == 0 else rows
    if parts * rows * width * (len(views) + 1) <= 4 << 20:
        tile = rows
    found = pl.pallas_call(
        lambda *refs: sum_split_kernel(len(views), *refs),
        grid_spec=pltpu.PrefetchScalarGridSpec(
            num_scalar_prefetch=1,
            grid=(lead, rows // tile),
            in_specs=[pl.BlockSpec((1, parts, tile, width), lambda a, r, _: (a, 0, r, 0))]
            * len(views),
            out_specs=[pl.BlockSpec((1, tile, width), lambda a, r, _: (a, r, 0))] * parts,
        ),
        out_shape=[jax.ShapeDtypeStruct((lead, rows, width), BF)] * parts,
        name="sum_split",
    )(place.reshape((1,)).astype(jnp.int32), *views)
    return [found[0]] + [
        lax.ppermute(found[shift], axis, factor_pairs(size, stride, parts, shift))
        for shift in range(1, parts)
    ]


def second_stage(arrays, order):
    groups, outer = arrays[0].shape[:2]
    inner = factors("tensor")[1]
    far, near = factors("dp")
    if order == "tensor first":
        return stage(arrays, groups, "tensor", inner, outer)
    return stage(arrays, far, "dp", 1, near)


def third_stage(arrays, order):
    outer, inner = factors("tensor")
    far, near = factors("dp")
    if order == "tensor first":
        return stage(arrays, far, "dp", 1, near)
    return stage(arrays, far, "tensor", inner, outer)


def last_stage(arrays):
    far, near = factors("dp")
    arrays = stage(arrays, 1, "dp", near, far)
    total = arrays[0][0].astype(F32)
    for item in arrays[1:]:
        total = total + item[0].astype(F32)
    return total


def split_high_low(values):
    high = values.astype(BF)
    return high, (values - high.astype(F32)).astype(BF)


def body(
    tokens,
    segments,
    expert_ids,
    cotangent,
    attn_gain,
    ffn_gain,
    latent_gain,
    latent_down,
    router_proj,
    query_proj,
    kv_expand,
    output_proj,
    shared_gate,
    shared_up,
    shared_down,
    experts,
):
    both = ("dp", "tensor")
    n_dp, n_tensor = lax.axis_size("dp"), lax.axis_size("tensor")
    n_all = n_dp * n_tensor
    dp_index, tensor_index = lax.axis_index("dp"), lax.axis_index("tensor")
    own_rows, model_width = tokens.shape
    count = own_rows * n_tensor
    first_row = tensor_index * own_rows
    down_rows, lat_rope = latent_down.shape
    local_experts = experts.shape[0]
    capacity = count * TOPK * 4 // (3 * EXPERTS)
    slots = local_experts * capacity
    doc_ids = segments[0]

    small_width = lat_rope + EXPERTS
    own_ids = lax.dynamic_slice_in_dim(expert_ids, first_row, own_rows, 0)
    gain_piece, lat_piece = attn_gain.shape[0], latent_gain.shape[0]
    gain_row = jnp.concatenate([attn_gain, ffn_gain, latent_gain])
    gain_row = jnp.pad(gain_row, (0, small_width - gain_row.shape[0]))[None]
    id_rows = -(-own_rows * TOPK // small_width)
    ids_flat = own_ids.astype(BF).reshape(-1)
    ids_flat = jnp.pad(ids_flat, (0, id_rows * small_width - ids_flat.shape[0]))
    extra_rows = -(-(1 + id_rows) // 16) * 16
    small = jnp.concatenate(
        [
            jnp.concatenate([latent_down, router_proj], axis=1),
            gain_row,
            ids_flat.reshape((id_rows, small_width)),
            jnp.zeros((extra_rows - 1 - id_rows, small_width), BF),
        ],
        axis=0,
    )
    small_four = lax.all_gather(small, "tensor", axis=0, tiled=True)
    tokens_in, _ = lax.optimization_barrier((tokens, small_four))
    rows_all = row_major(lax.all_gather(row_major(tokens_in), "tensor", axis=0, tiled=True))
    small_all = gather_rows(small_four, "dp").reshape(
        (n_all, down_rows + extra_rows, small_width)
    )
    query_full = gather_rows(query_proj, "dp")
    expand_full = gather_rows(kv_expand, "dp")
    out_full = gather_rows(output_proj, "dp")
    cot_in, _, _ = lax.optimization_barrier((cotangent, query_full, expand_full))
    cot_all = row_major(lax.all_gather(row_major(cot_in), both, axis=0, tiled=True))
    down_router = small_all[:, :down_rows].reshape((n_all * down_rows, small_width))
    down_full = down_router[:, :lat_rope]
    router_full = down_router[:, lat_rope:]
    gains = small_all[:, down_rows].astype(F32)
    gain_one = gains[:, :gain_piece].reshape(-1)
    gain_two = gains[:, gain_piece : 2 * gain_piece].reshape(-1)
    gain_lat = gains[:, 2 * gain_piece : 2 * gain_piece + lat_piece].reshape(-1)
    ids_all = (
        small_all[:, down_rows + 1 : down_rows + 1 + id_rows]
        .reshape((n_all, id_rows * small_width))[:, : own_rows * TOPK]
        .astype(jnp.int32)
        .reshape((n_dp, count, TOPK))
    )

    first_expert = dp_index * local_experts
    here = first_expert + jnp.arange(local_experts, dtype=jnp.int32)
    named = jnp.any(ids_all[:, None, :, :] == here[None, :, None, None], axis=-1)
    token_pos = jnp.arange(count, dtype=jnp.int32)
    earlier = (token_pos[:, None] < token_pos[None, :]).astype(BF)
    position = lax.dot_general(
        named.astype(BF).reshape((n_dp * local_experts, count)),
        earlier,
        (((1,), (0,)), ((), ())),
        preferred_element_type=F32,
    ).reshape((n_dp, local_experts, count))
    position = jnp.where(named, position, -1.0)
    every = jnp.arange(EXPERTS, dtype=jnp.int32)
    spare = -(-EXPERTS // 128) * 128
    chosen_mask = jnp.any(ids_all[:, :, :, None] == every[None, None, None, :], axis=2).astype(F32)
    mask_wide = jnp.pad(chosen_mask, ((0, 0), (0, 0), (0, spare - EXPERTS)))
    router_wide = jnp.pad(router_full, ((0, 0), (0, spare - EXPERTS)))

    width_q = NOPE + ROPE
    local_heads = query_full.shape[1] // width_q
    cosines, sines = rope_tables(count, ROPE)
    residual = rows_all.astype(F32)
    inv_one = rms_scale(residual)
    normed_one = (residual * inv_one * gain_one).astype(BF)
    latent = jnp.dot(normed_one, down_full, preferred_element_type=F32)
    query = jnp.dot(normed_one, query_full, preferred_element_type=F32).reshape(
        (count, local_heads, width_q)
    )
    compressed = latent[:, :LAT]
    inv_lat = rms_scale(compressed)
    comp_normed = (compressed * inv_lat * gain_lat).astype(BF)
    expanded = jnp.dot(comp_normed, expand_full, preferred_element_type=F32).reshape(
        (count, local_heads, NOPE + VDIM)
    )
    query_rot = rotate(query[:, :, NOPE:], cosines[:, None, :], sines[:, None, :])
    key_rot = rotate(latent[:, LAT:], cosines, sines)
    query_all = jnp.concatenate([query[:, :, :NOPE], query_rot], axis=-1).astype(BF)
    key_all = jnp.concatenate(
        [expanded[:, :, :NOPE], jnp.broadcast_to(key_rot[:, None, :], (count, local_heads, ROPE))],
        axis=-1,
    ).astype(BF)
    value_all = expanded[:, :, NOPE:].astype(BF)
    context, log_total = attend(query_all, key_all, value_all, doc_ids)
    context_b = context.reshape((count, local_heads * VDIM)).astype(BF)
    attn_own = scatter_rows(matmul_t(context_b, out_full), "tensor")
    middle = tokens.astype(F32) + attn_own
    inv_two = rms_scale(middle)
    normed_two_own = (middle * inv_two * gain_two).astype(BF)
    normed_sent, cot_all = lax.optimization_barrier((row_major(normed_two_own), cot_all))
    normed_all = row_major(lax.all_gather(normed_sent, both, axis=0, tiled=True))
    sff = shared_gate.shape[1]
    shared_mine = jnp.concatenate(
        [jnp.transpose(shared_gate), jnp.transpose(shared_up), jnp.transpose(shared_down)], axis=0
    )
    shared_mine, _ = lax.optimization_barrier((shared_mine, normed_all))
    shared_full = gather_columns(shared_mine, "dp")
    sgate_full = shared_full[:sff]
    sup_full = shared_full[sff : 2 * sff]
    sdown_full = shared_full[2 * sff :]


    experts_t = jnp.swapaxes(experts, 2, 3)
    first = first_expert.reshape((1,)).astype(jnp.int32)
    grads_disp = dispatch(position, cot_all, capacity)
    rows_disp, slot_w = dispatch_route(
        first, position, normed_all, mask_wide, router_wide, capacity
    )
    out_a, out_b, back_a, back_b, saved = expert_math(
        first, rows_disp, grads_disp, experts_t, slot_w, spare
    )
    half = model_width // 2
    back_a = second_stage(core_stage(position, back_a), "tensor first")
    back_b = second_stage(core_stage(position, back_b), "dp first")
    out_a, out_b, saved, _, _ = lax.optimization_barrier(
        (out_a, out_b, saved, back_a[0], back_b[0])
    )
    grad_experts = jnp.swapaxes(expert_grads(rows_disp, grads_disp, saved), 2, 3)
    out_a = core_stage(position, out_a)
    out_b = core_stage(position, out_b)
    back_a = third_stage(back_a, "tensor first")
    back_b = third_stage(back_b, "dp first")
    back_mark = (back_a[0], back_b[0])
    back_own_a, back_own_b = last_stage(back_a), last_stage(back_b)
    out_a, out_b, _, _ = lax.optimization_barrier((out_a, out_b, back_own_a, back_own_b))
    out_a = third_stage(second_stage(out_a, "tensor first"), "tensor first")
    out_b = third_stage(second_stage(out_b, "dp first"), "dp first")
    out_own_a, out_own_b = last_stage(out_a), last_stage(out_b)

    seq_row = dp_index * count
    normed_two = lax.dynamic_slice_in_dim(normed_all, seq_row, count, 0)
    grad_all = lax.dynamic_slice_in_dim(cot_all, seq_row, count, 0)
    shared_pre_gate = matmul_t(normed_two, sgate_full)
    shared_pre_up = matmul_t(normed_two, sup_full)
    sigma_shared = jax.nn.sigmoid(shared_pre_gate)
    shared_hidden = (shared_pre_gate * sigma_shared * shared_pre_up).astype(BF)
    d_shared = matmul_t(grad_all, sdown_full)
    d_sgate = (
        d_shared * shared_pre_up * sigma_shared * (1.0 + shared_pre_gate * (1.0 - sigma_shared))
    ).astype(BF)
    d_sup = (d_shared * shared_pre_gate * sigma_shared).astype(BF)
    d_shared_own = scatter_rows(dot_nn(d_sgate, sgate_full) + dot_nn(d_sup, sup_full), "tensor")
    shared_own = scatter_rows(dot_nn(shared_hidden, sdown_full), "tensor")
    shared_lefts, _ = lax.optimization_barrier(((d_sgate, d_sup, shared_hidden), back_mark))
    shared_grads = scatter_products(shared_lefts, [normed_two, normed_two, grad_all], "dp")
    block_out = middle + shared_own + jnp.concatenate([out_own_a, out_own_b], axis=1)

    own_first = seq_row + first_row
    d_weight = back_own_b[:, half : half + EXPERTS]
    mask_own = lax.dynamic_slice_in_dim(
        chosen_mask.reshape((n_dp * count, EXPERTS)), own_first, own_rows, 0
    )
    scores_own = jax.nn.sigmoid(dot_nn(normed_two_own, router_full))
    chosen_own = scores_own * mask_own
    total_own = jnp.sum(chosen_own, axis=1, keepdims=True)
    d_chosen = route_scale * (
        d_weight / total_own
        - jnp.sum(d_weight * chosen_own, axis=1, keepdims=True) / (total_own * total_own)
    )
    d_logits = (d_chosen * mask_own * scores_own * (1.0 - scores_own)).astype(BF)
    d_normed_two = (
        d_shared_own
        + jnp.concatenate([back_own_a, back_own_b[:, :half]], axis=1)
        + matmul_t(d_logits, router_full)
    )
    grad_gain_two = jnp.sum(d_normed_two * middle * inv_two, axis=0)
    d_middle = cotangent.astype(F32) + norm_back(d_normed_two, middle, inv_two, gain_two)
    two_high, two_low = split_high_low(grad_gain_two)
    mid_sent = jnp.concatenate(
        [
            jnp.concatenate(
                [d_middle.astype(BF), jnp.pad(d_logits, ((0, 0), (0, spare - EXPERTS)))], axis=1
            ),
            jnp.pad(jnp.stack([two_high, two_low]), ((0, 14), (0, spare))),
        ],
        axis=0,
    )
    mid_all = gather_rows(row_major(mid_sent), "tensor").reshape(
        (n_tensor, own_rows + 16, model_width + spare)
    )
    d_mid_b = mid_all[:, :own_rows, :model_width].reshape((count, model_width))
    d_logits_seq = mid_all[:, :own_rows, model_width : model_width + EXPERTS].reshape(
        (count, EXPERTS)
    )
    gain_two_sum = jnp.sum(mid_all[:, own_rows : own_rows + 2, :model_width].astype(F32), axis=(0, 1))
    grad_out = scatter_rows(matmul_tl(d_mid_b, context_b), "dp")
    d_context = (
        jnp.dot(d_mid_b, out_full, preferred_element_type=F32)
        .astype(BF)
        .reshape((count, local_heads, VDIM))
    )
    d_query, d_key, d_value = attend_back(
        query_all, key_all, value_all, doc_ids, log_total, d_context
    )
    d_query_rot = unrotate(d_query[:, :, NOPE:], cosines[:, None, :], sines[:, None, :])
    d_query_all = (
        jnp.concatenate([d_query[:, :, :NOPE], d_query_rot], axis=-1)
        .reshape((count, local_heads * width_q))
        .astype(BF)
    )
    d_expanded = (
        jnp.concatenate([d_key[:, :, :NOPE], d_value], axis=-1)
        .reshape((count, local_heads * (NOPE + VDIM)))
        .astype(BF)
    )
    d_key_rot = jnp.sum(d_key[:, :, NOPE:], axis=1)
    back_own = scatter_rows(
        jnp.concatenate(
            [
                matmul_t(d_query_all, query_full).astype(BF),
                matmul_t(d_expanded, expand_full).astype(BF),
                d_key_rot.astype(BF),
                jnp.zeros((count, ROPE), BF),
            ],
            axis=1,
        ),
        "tensor",
    )
    grad_query = scatter_rows(matmul_tl(normed_one, d_query_all), "dp")
    grad_expand = scatter_rows(matmul_tl(comp_normed, d_expanded), "dp")
    d_rows_query = back_own[:, :model_width]
    d_comp_own = back_own[:, model_width : model_width + LAT]
    d_rot_own = back_own[:, model_width + LAT : model_width + LAT + ROPE]
    seq_own = lambda values: lax.dynamic_slice_in_dim(values, first_row, own_rows, 0)
    compressed_own, inv_lat_own = seq_own(compressed), seq_own(inv_lat)
    grad_gain_lat = jnp.sum(d_comp_own * compressed_own * inv_lat_own, axis=0)
    d_comp = norm_back(d_comp_own, compressed_own, inv_lat_own, gain_lat)
    d_latent = jnp.concatenate(
        [d_comp, unrotate(d_rot_own, seq_own(cosines), seq_own(sines))], axis=-1
    ).astype(BF)
    lat_high, lat_low = split_high_low(grad_gain_lat)
    lat_sent = jnp.concatenate(
        [d_latent, jnp.pad(jnp.stack([lat_high, lat_low]), ((0, 14), (0, lat_rope - LAT)))], axis=0
    )
    lat_all = gather_rows(row_major(lat_sent), "tensor").reshape(
        (n_tensor, own_rows + 16, lat_rope)
    )
    d_latent_seq = lat_all[:, :own_rows].reshape((count, lat_rope))
    gain_lat_sum = jnp.sum(lat_all[:, own_rows : own_rows + 2, :LAT].astype(F32), axis=(0, 1))
    residual_own, inv_one_own = tokens.astype(F32), seq_own(inv_one)
    d_normed_one = d_rows_query + matmul_t(d_latent, down_full)
    grad_gain_one = jnp.sum(d_normed_one * residual_own * inv_one_own, axis=0)
    grad_tokens = d_middle + norm_back(d_normed_one, residual_own, inv_one_own, gain_one)
    gain_one_share = scatter_rows(
        jnp.swapaxes(grad_gain_one.reshape((n_dp, n_tensor, gain_piece)), 0, 1), "tensor"
    )[0]

    def own_share(values, piece):
        view = values.reshape((n_dp, n_tensor, piece) + values.shape[1:])
        return pick(view, tensor_index, 1)

    wide = jnp.concatenate(
        [
            own_share(matmul_tl(normed_one, d_latent_seq), down_rows),
            own_share(matmul_tl(normed_two, d_logits_seq), down_rows),
        ],
        axis=2,
    )
    gain_line = jnp.concatenate(
        [gain_one_share, own_share(gain_two_sum, gain_piece), own_share(gain_lat_sum, lat_piece)],
        axis=1,
    )
    gain_line = jnp.pad(
        gain_line[:, None, :], ((0, 0), (0, 15), (0, small_width - 2 * gain_piece - lat_piece))
    )
    small_sum = scatter_rows(
        jnp.concatenate([wide, gain_line], axis=1).reshape((n_dp * (down_rows + 16), small_width)),
        "dp",
    )
    gain_out = small_sum[down_rows]
    return (
        block_out,
        grad_tokens,
        gain_out[:gain_piece],
        gain_out[gain_piece : 2 * gain_piece],
        gain_out[2 * gain_piece : 2 * gain_piece + lat_piece],
        small_sum[:down_rows, :lat_rope],
        small_sum[:down_rows, lat_rope:],
        grad_query,
        grad_expand,
        grad_out,
        jnp.transpose(shared_grads[:sff]),
        jnp.transpose(shared_grads[sff : 2 * sff]),
        jnp.transpose(shared_grads[2 * sff :]),
        grad_experts,
    )


def solution(mesh):
    in_specs = (
        P(("dp", "tensor"), None),
        P("dp", None),
        P("dp", None),
        P(("dp", "tensor"), None),
        P(("dp", "tensor")),
        P(("dp", "tensor")),
        P(("dp", "tensor")),
        P(("dp", "tensor"), None),
        P(("dp", "tensor"), None),
        P("dp", "tensor"),
        P("dp", "tensor"),
        P("dp", "tensor"),
        P("dp", "tensor"),
        P("dp", "tensor"),
        P("dp", "tensor"),
        P("dp", None, None, "tensor"),
    )
    out_specs = (
        P(("dp", "tensor"), None),
        P(("dp", "tensor"), None),
        P(("dp", "tensor")),
        P(("dp", "tensor")),
        P(("dp", "tensor")),
        P(("dp", "tensor"), None),
        P(("dp", "tensor"), None),
        P("dp", "tensor"),
        P("dp", "tensor"),
        P("dp", "tensor"),
        P("dp", "tensor"),
        P("dp", "tensor"),
        P("dp", "tensor"),
        P("dp", None, None, "tensor"),
    )
    return jax.shard_map(body, mesh=mesh, in_specs=in_specs, out_specs=out_specs, check_vma=False)
```

```python
import math

import jax
import jax.numpy as jnp
from jax import lax
from jax.experimental import pallas as pl
from jax.experimental.pallas import tpu as pltpu
from jax.experimental.layout import Layout, with_layout_constraint
from jax.sharding import PartitionSpec as P

NOPE = 128
ROPE = 64
VDIM = 128
LAT = 512
EXPERTS = 64
TOPK = 6


eps = 1e-06
route_scale = 2.446
rope_base = 50000.0


def rms_scale(values):
    return lax.rsqrt(jnp.mean(values * values, axis=-1, keepdims=True) + eps)


def norm_back(grad_normed, values, inverse, gain):
    scaled = grad_normed * gain
    return inverse * scaled - values * inverse * inverse * inverse * jnp.mean(
        scaled * values, axis=-1, keepdims=True
    )


def rope_tables(count, width):
    half = width // 2
    powers = jnp.arange(half, dtype=jnp.int32).astype(jnp.float32) * (2.0 / width)
    freqs = jnp.exp(-math.log(rope_base) * powers)
    angles = jnp.arange(count, dtype=jnp.int32).astype(jnp.float32)[:, None] * freqs[None, :]
    return (jnp.cos(angles), jnp.sin(angles))


def rotate(values, cosines, sines):
    half = values.shape[-1] // 2
    first = values[..., :half]
    second = values[..., half:]
    return jnp.concatenate(
        [first * cosines - second * sines, second * cosines + first * sines], axis=-1
    )


def unrotate(grads, cosines, sines):
    half = grads.shape[-1] // 2
    first = grads[..., :half]
    second = grads[..., half:]
    return jnp.concatenate(
        [first * cosines + second * sines, second * cosines - first * sines], axis=-1
    )


def matmul_t(left, right):
    return lax.dot_general(
        left, right, (((1,), (1,)), ((), ())), preferred_element_type=jnp.float32
    )


def matmul_tl(left, right):
    return lax.dot_general(
        left, right, (((0,), (0,)), ((), ())), preferred_element_type=jnp.float32
    )


def attend(query_all, key_all, value_all, doc_ids):
    count = query_all.shape[0]
    block = min(512, count)
    scale = 1.0 / math.sqrt(query_all.shape[-1])
    key_pos = jnp.arange(count, dtype=jnp.int32)

    def one_block(begin):
        query_pos = begin + jnp.arange(block, dtype=jnp.int32)
        allowed = (doc_ids[:, None] == doc_ids[None, :]) & (key_pos[None, :] <= query_pos[:, None])
        scores = (
            jnp.einsum("qhc,khc->hqk", query_all, key_all, preferred_element_type=jnp.float32)
            * scale
        )
        raw_weights = jnp.where(allowed[None], jnp.exp(scores), 0.0)
        total = jnp.sum(raw_weights, axis=-1)
        probs = (raw_weights / total[..., None]).astype(jnp.bfloat16)
        context = jnp.einsum("hqk,khc->qhc", probs, value_all, preferred_element_type=jnp.float32)
        return (context, jnp.log(total))

    begins = jnp.arange(0, count, block, dtype=jnp.int32)
    contexts, logs = lax.map(one_block, begins)
    heads = query_all.shape[1]
    context = contexts.reshape((count, heads, value_all.shape[2]))
    log_total = jnp.transpose(logs, (1, 0, 2)).reshape((heads, count))
    return (context, log_total)


def attend_back(query_all, key_all, value_all, doc_ids, log_total, d_context):
    count = query_all.shape[0]
    heads = query_all.shape[1]
    block = min(512, count)
    scale = 1.0 / math.sqrt(query_all.shape[-1])
    key_pos = jnp.arange(count, dtype=jnp.int32)

    def one_block(carry, begin):
        d_keys, d_values = carry
        query_pos = begin + jnp.arange(block, dtype=jnp.int32)
        allowed = (doc_ids[:, None] == doc_ids[None, :]) & (key_pos[None, :] <= query_pos[:, None])
        scores = (
            jnp.einsum("qhc,khc->hqk", query_all, key_all, preferred_element_type=jnp.float32)
            * scale
        )
        probs = jnp.where(allowed[None], jnp.exp(scores - log_total[..., None]), 0.0)
        d_values = d_values + jnp.einsum(
            "hqk,qhc->khc",
            probs.astype(jnp.bfloat16),
            d_context,
            preferred_element_type=jnp.float32,
        )
        d_probs = jnp.einsum(
            "qhc,khc->hqk", d_context, value_all, preferred_element_type=jnp.float32
        )
        delta = jnp.sum(probs * d_probs, axis=-1, keepdims=True)
        d_scores = (probs * (d_probs - delta) * scale).astype(jnp.bfloat16)
        d_queries = jnp.einsum(
            "hqk,khc->qhc", d_scores, key_all, preferred_element_type=jnp.float32
        )
        d_keys = d_keys + jnp.einsum(
            "hqk,qhc->khc", d_scores, query_all, preferred_element_type=jnp.float32
        )
        return ((d_keys, d_values), d_queries)

    begins = jnp.arange(0, count, block, dtype=jnp.int32)
    start_state = (jnp.zeros(key_all.shape, jnp.float32), jnp.zeros(value_all.shape, jnp.float32))
    (d_keys, d_values), d_queries = lax.scan(one_block, start_state, begins)
    return (d_queries.reshape((count, heads, query_all.shape[2])), d_keys, d_values)


BF = jnp.bfloat16
F32 = jnp.float32


def row_major(array):
    return with_layout_constraint(array, Layout(major_to_minor=tuple(range(array.ndim))))


def factor_pairs(size, stride, parts, shift):
    pairs = []
    for index in range(size):
        place = index // stride % parts
        pairs.append((index, index + ((place + shift) % parts - place) * stride))
    return pairs


def pick(array, index, dim):
    return lax.dynamic_index_in_dim(array, index, dim, keepdims=False)


def scatter_factor(array, dim, axis, stride, parts, final=False):
    size = lax.axis_size(axis)
    place = lax.axis_index(axis) // stride % parts
    received = [
        lax.ppermute(
            pick(array, (place + shift) % parts, dim),
            axis,
            factor_pairs(size, stride, parts, shift),
        )
        for shift in range(1, parts)
    ]
    total = pick(array, place, dim).astype(F32)
    for item in received:
        total = total + item.astype(F32)
    return total if final else total.astype(BF)


def factors(axis):
    size = lax.axis_size(axis)
    inner = 2 if size % 2 == 0 else 1
    return size // inner, inner


def gather_pieces(shard, axis):
    size = lax.axis_size(axis)
    outer, inner = factors(axis)
    index = lax.axis_index(axis)
    far, near = index // inner, index % inner
    pieces = [shard] + [
        lax.ppermute(shard, axis, factor_pairs(size, inner, outer, shift))
        for shift in range(1, outer)
    ]
    found = []
    for shift, piece in enumerate(pieces):
        source = (far - shift) % outer
        found.append((source, near, piece))
        for turn in range(1, inner):
            other = lax.ppermute(piece, axis, factor_pairs(size, 1, inner, turn))
            found.append((source, (near - turn) % inner, other))
    return found


def gather_rows(shard, axis):
    inner = factors(axis)[1]
    rows = shard.shape[0]
    full = jnp.zeros((lax.axis_size(axis) * rows,) + shard.shape[1:], shard.dtype)
    rest = (0,) * (shard.ndim - 1)
    for far, near, piece in gather_pieces(shard, axis):
        full = lax.dynamic_update_slice(full, piece, ((far * inner + near) * rows,) + rest)
    return full


def scatter_rows(array, axis, final=True):
    outer, inner = factors(axis)
    rows = array.shape[0] // (outer * inner)
    view = row_major(array.astype(BF)).reshape((outer, inner, rows) + array.shape[1:])
    view = scatter_factor(view, 1, axis, 1, inner)
    return scatter_factor(view, 0, axis, inner, outer, final)


def scatter_products(lefts, rights, axis):
    size = lax.axis_size(axis)
    blocks = jnp.concatenate(
        [matmul_tl(left, right).astype(BF) for left, right in zip(lefts, rights)], axis=0
    )
    rows, columns = blocks.shape[0], blocks.shape[1] // size
    blocks = jnp.swapaxes(blocks.reshape((rows, size, columns)), 0, 1)
    blocks = row_major(blocks.reshape((size * rows, columns)))
    return lax.psum_scatter(blocks, axis, scatter_dimension=0, tiled=True).astype(F32)


def dot_nn(left, right):
    return lax.dot_general(left, right, (((1,), (0,)), ((), ())), preferred_element_type=F32)


def place_of(position_ref, capacity):
    _, count, tokens = position_ref.shape
    slot = lax.broadcasted_iota(jnp.int32, (capacity, tokens), 0).astype(F32)
    return jnp.concatenate(
        [
            jnp.where(position_ref[0, e : e + 1, :] == slot, 1.0, 0.0).astype(BF)
            for e in range(count)
        ],
        axis=0,
    )


def dispatch_kernel(position_ref, rows_ref, out_ref):
    place = place_of(position_ref, out_ref.shape[2])
    out_ref[...] = dot_nn(place, rows_ref[0]).astype(BF).reshape(out_ref.shape)


def route_kernel(first_ref, position_ref, rows_ref, mask_ref, router_ref, out_ref, slot_w_ref):
    _, count, capacity, width = out_ref.shape
    place = place_of(position_ref, capacity)
    rows = rows_ref[0]
    out_ref[...] = dot_nn(place, rows).astype(BF).reshape(out_ref.shape)
    chosen = jax.nn.sigmoid(dot_nn(rows, router_ref[...])) * mask_ref[0]
    weights = route_scale * chosen / jnp.sum(chosen, axis=1, keepdims=True)
    high = weights.astype(BF)
    low = (weights - high.astype(F32)).astype(BF)
    spread = dot_nn(place, high) + dot_nn(place, low)
    lane = lax.broadcasted_iota(jnp.int32, spread.shape, 1)
    slot_expert = lax.broadcasted_iota(jnp.int32, spread.shape, 0) // capacity + first_ref[0]
    mine = jnp.sum(jnp.where(lane == slot_expert, spread, 0.0), axis=1, keepdims=True)
    slot_w_ref[...] = jnp.broadcast_to(mine, spread.shape).reshape(slot_w_ref.shape)


def dispatch(position, rows, capacity):
    groups, count, tokens = position.shape
    width = rows.shape[1]
    return pl.pallas_call(
        dispatch_kernel,
        grid=(groups,),
        in_specs=[
            pl.BlockSpec((1, count, tokens), lambda s: (s, 0, 0)),
            pl.BlockSpec((1, tokens, width), lambda s: (s, 0, 0)),
        ],
        out_specs=pl.BlockSpec((1, count, capacity, width), lambda s: (s, 0, 0, 0)),
        out_shape=jax.ShapeDtypeStruct((groups, count, capacity, width), BF),
        name="dispatch",
    )(position, rows.reshape((groups, tokens, width)))


def dispatch_route(first, position, rows, mask, router, capacity):
    groups, count, tokens = position.shape
    width = rows.shape[1]
    lanes = router.shape[1]
    slab = lambda cols: pl.BlockSpec((1, count, capacity, cols), lambda s, _: (s, 0, 0, 0))
    return pl.pallas_call(
        route_kernel,
        grid_spec=pltpu.PrefetchScalarGridSpec(
            num_scalar_prefetch=1,
            grid=(groups,),
            in_specs=[
                pl.BlockSpec((1, count, tokens), lambda s, _: (s, 0, 0)),
                pl.BlockSpec((1, tokens, width), lambda s, _: (s, 0, 0)),
                pl.BlockSpec((1, tokens, lanes), lambda s, _: (s, 0, 0)),
                pl.BlockSpec((width, lanes), lambda s, _: (0, 0)),
            ],
            out_specs=[slab(width), slab(lanes)],
        ),
        out_shape=[
            jax.ShapeDtypeStruct((groups, count, capacity, width), BF),
            jax.ShapeDtypeStruct((groups, count, capacity, lanes), F32),
        ],
        name="dispatch_route",
    )(first, position, rows.reshape((groups, tokens, width)), mask, router)


def expert_kernel(
    first_ref, rows_ref, grads_ref, weights_ref, slot_w_ref,
    out_a_ref, out_b_ref, back_a_ref, back_b_ref, saved_ref,
):
    groups, _, capacity, width = rows_ref.shape
    slots = groups * capacity
    rows = rows_ref[...].reshape((slots, width))
    grads = grads_ref[...].reshape((slots, width))
    gate = matmul_t(rows, weights_ref[0, 0])
    up = matmul_t(rows, weights_ref[0, 1])
    d_plain = matmul_t(grads, weights_ref[0, 2])
    slot_w = slot_w_ref[...].reshape((slots, slot_w_ref.shape[-1]))[:, :1]
    sigma = jax.nn.sigmoid(gate)
    silu = gate * sigma
    hidden = silu * up
    d_weight = jnp.sum(hidden * d_plain, axis=1, keepdims=True)
    hidden_w = (hidden * slot_w).astype(BF)
    d_hidden = d_plain * slot_w
    d_gate = (d_hidden * up * sigma * (1.0 + gate * (1.0 - sigma))).astype(BF)
    d_up = (d_hidden * silu).astype(BF)
    saved_ref[0, 0] = d_gate
    saved_ref[0, 1] = d_up
    saved_ref[0, 2] = hidden_w
    half = out_a_ref.shape[-1]
    shape_half = (groups, 1, capacity, half)
    for part, out_ref, back_ref in ((0, out_a_ref, back_a_ref), (1, out_b_ref, back_b_ref)):
        cols = pl.ds(part * half, half)
        back = dot_nn(d_gate, weights_ref[0, 0, :, cols]) + dot_nn(
            d_up, weights_ref[0, 1, :, cols]
        )
        back_ref[:, :, :, :half] = back.astype(BF).reshape(shape_half)
        out_ref[...] = dot_nn(hidden_w, weights_ref[0, 2, :, cols]).astype(BF).reshape(shape_half)
    spare = back_b_ref.shape[-1] - half
    lane = lax.broadcasted_iota(jnp.int32, (slots, spare), 1)
    spread = jnp.where(lane == first_ref[0] + pl.program_id(0), d_weight, 0.0)
    back_b_ref[:, :, :, half:] = spread.astype(BF).reshape((groups, 1, capacity, spare))


def group_tile(groups, capacity):
    return max(t for t in range(1, groups + 1) if groups % t == 0 and t * capacity <= 512)


def expert_math(first, rows, grads, experts_t, slot_w, spare):
    groups, count, capacity, width = rows.shape
    hidden = experts_t.shape[2]
    tile = group_tile(groups, capacity)
    half = width // 2
    slab = lambda cols: pl.BlockSpec((tile, 1, capacity, cols), lambda e, s, _: (s, e, 0, 0))
    shape = lambda cols: jax.ShapeDtypeStruct((groups, count, capacity, cols), BF)
    slots = groups * capacity
    return pl.pallas_call(
        expert_kernel,
        grid_spec=pltpu.PrefetchScalarGridSpec(
            num_scalar_prefetch=1,
            grid=(count, groups // tile),
            in_specs=[
                slab(width),
                slab(width),
                pl.BlockSpec((1, 3, hidden, width), lambda e, s, _: (e, 0, 0, 0)),
                slab(slot_w.shape[-1]),
            ],
            out_specs=[
                slab(half),
                slab(half),
                slab(half),
                slab(half + spare),
                pl.BlockSpec((1, 3, tile * capacity, hidden), lambda e, s, _: (e, 0, s, 0)),
            ],
        ),
        out_shape=[
            shape(half),
            shape(half),
            shape(half),
            shape(half + spare),
            jax.ShapeDtypeStruct((count, 3, slots, hidden), BF),
        ],
        compiler_params=pltpu.CompilerParams(vmem_limit_bytes=60 * 1024 * 1024),
        name="expert_math",
    )(first, rows, grads, experts_t, slot_w)


def expert_grad_kernel(rows_ref, grads_ref, saved_ref, out_ref):
    groups, _, capacity, width = rows_ref.shape
    slots = groups * capacity
    rows = rows_ref[...].reshape((slots, width))
    grads = grads_ref[...].reshape((slots, width))
    found = (
        matmul_tl(saved_ref[0, 0], rows),
        matmul_tl(saved_ref[0, 1], rows),
        matmul_tl(saved_ref[0, 2], grads),
    )

    @pl.when(pl.program_id(1) == 0)
    def _():
        for which in range(3):
            out_ref[0, which] = found[which]

    @pl.when(pl.program_id(1) > 0)
    def _():
        for which in range(3):
            out_ref[0, which] += found[which]


def expert_grads(rows, grads, saved):
    groups, count, capacity, width = rows.shape
    hidden = saved.shape[3]
    tile = group_tile(groups, capacity)
    slab = pl.BlockSpec((tile, 1, capacity, width), lambda e, s: (s, e, 0, 0))
    return pl.pallas_call(
        expert_grad_kernel,
        grid=(count, groups // tile),
        in_specs=[
            slab,
            slab,
            pl.BlockSpec((1, 3, tile * capacity, hidden), lambda e, s: (e, 0, s, 0)),
        ],
        out_specs=pl.BlockSpec((1, 3, hidden, width), lambda e, s: (e, 0, 0, 0)),
        out_shape=jax.ShapeDtypeStruct((count, 3, hidden, width), F32),
        compiler_params=pltpu.CompilerParams(vmem_limit_bytes=60 * 1024 * 1024),
        name="expert_grads",
    )(rows, grads, saved)


def combine_kernel(core_ref, position_ref, values_ref, keep_ref, send_ref):
    _, count, capacity, width = values_ref.shape
    tokens = position_ref.shape[2]
    own = tokens // (2 * keep_ref.shape[1])
    place = place_of(position_ref, capacity)
    found = matmul_tl(place, values_ref[...].reshape((count * capacity, width))).astype(BF)
    found = found.reshape((keep_ref.shape[1], 2, own, width))
    for core in range(2):

        @pl.when(core_ref[0] == core)
        def _():
            keep_ref[0] = found[:, core]
            send_ref[0] = found[:, 1 - core]


def core_stage(position, values):
    groups, count, tokens = position.shape
    capacity, width = values.shape[2:]
    size = lax.axis_size("tensor")
    outer, inner = factors("tensor")
    own = tokens // size
    core = lax.axis_index("tensor") % inner
    slab = pl.BlockSpec((1, outer, own, width), lambda s, _: (s, 0, 0, 0))
    shape = jax.ShapeDtypeStruct((groups, outer, own, width), BF)
    keep, send = pl.pallas_call(
        combine_kernel,
        grid_spec=pltpu.PrefetchScalarGridSpec(
            num_scalar_prefetch=1,
            grid=(groups,),
            in_specs=[
                pl.BlockSpec((1, count, tokens), lambda s, _: (s, 0, 0)),
                pl.BlockSpec((1, count, capacity, width), lambda s, _: (s, 0, 0, 0)),
            ],
            out_specs=[slab, slab],
        ),
        out_shape=[shape, shape],
        name="combine",
    )(core.reshape((1,)).astype(jnp.int32), position, values)
    return [keep, lax.ppermute(send, "tensor", factor_pairs(size, 1, inner, 1))]


def sum_split_kernel(count, place_ref, *refs):
    parts = refs[0].shape[1]
    for shift, out_ref in enumerate(refs[count:]):
        index = lax.rem(place_ref[0] + shift, parts)
        total = refs[0][0, index].astype(F32)
        for ref in refs[1:count]:
            total = total + ref[0, index].astype(F32)
        out_ref[0] = total.astype(BF)


def stage(arrays, lead, axis, stride, parts):
    width = arrays[0].shape[-1]
    size = lax.axis_size(axis)
    place = lax.axis_index(axis) // stride % parts
    rows = arrays[0].size // (lead * parts * width)
    views = [array.reshape((lead, parts, rows, width)) for array in arrays]
    tile = 32 if rows % 32 == 0 else rows
    if parts * rows * width * (len(views) + 1) <= 4 << 20:
        tile = rows
    found = pl.pallas_call(
        lambda *refs: sum_split_kernel(len(views), *refs),
        grid_spec=pltpu.PrefetchScalarGridSpec(
            num_scalar_prefetch=1,
            grid=(lead, rows // tile),
            in_specs=[pl.BlockSpec((1, parts, tile, width), lambda a, r, _: (a, 0, r, 0))]
            * len(views),
            out_specs=[pl.BlockSpec((1, tile, width), lambda a, r, _: (a, r, 0))] * parts,
        ),
        out_shape=[jax.ShapeDtypeStruct((lead, rows, width), BF)] * parts,
        name="sum_split",
    )(place.reshape((1,)).astype(jnp.int32), *views)
    return [found[0]] + [
        lax.ppermute(found[shift], axis, factor_pairs(size, stride, parts, shift))
        for shift in range(1, parts)
    ]


def second_stage(arrays, order):
    groups, outer = arrays[0].shape[:2]
    inner = factors("tensor")[1]
    far, near = factors("dp")
    if order == "tensor first":
        return stage(arrays, groups, "tensor", inner, outer)
    return stage(arrays, far, "dp", 1, near)


def third_stage(arrays, order):
    outer, inner = factors("tensor")
    far, near = factors("dp")
    if order == "tensor first":
        return stage(arrays, far, "dp", 1, near)
    return stage(arrays, far, "tensor", inner, outer)


def last_stage(arrays):
    far, near = factors("dp")
    arrays = stage(arrays, 1, "dp", near, far)
    total = arrays[0][0].astype(F32)
    for item in arrays[1:]:
        total = total + item[0].astype(F32)
    return total


def split_high_low(values):
    high = values.astype(BF)
    return high, (values - high.astype(F32)).astype(BF)


def body(
    tokens,
    segments,
    expert_ids,
    cotangent,
    attn_gain,
    ffn_gain,
    latent_gain,
    latent_down,
    router_proj,
    query_proj,
    kv_expand,
    output_proj,
    shared_gate,
    shared_up,
    shared_down,
    experts,
):
    both = ("dp", "tensor")
    n_dp, n_tensor = lax.axis_size("dp"), lax.axis_size("tensor")
    n_all = n_dp * n_tensor
    dp_index, tensor_index = lax.axis_index("dp"), lax.axis_index("tensor")
    own_rows, model_width = tokens.shape
    count = own_rows * n_tensor
    first_row = tensor_index * own_rows
    down_rows, lat_rope = latent_down.shape
    local_experts = experts.shape[0]
    capacity = count * TOPK * 4 // (3 * EXPERTS)
    slots = local_experts * capacity
    doc_ids = segments[0]

    small_width = lat_rope + EXPERTS
    own_ids = lax.dynamic_slice_in_dim(expert_ids, first_row, own_rows, 0)
    gain_piece, lat_piece = attn_gain.shape[0], latent_gain.shape[0]
    gain_row = jnp.concatenate([attn_gain, ffn_gain, latent_gain])
    gain_row = jnp.pad(gain_row, (0, small_width - gain_row.shape[0]))[None]
    id_rows = -(-own_rows * TOPK // small_width)
    ids_flat = own_ids.astype(BF).reshape(-1)
    ids_flat = jnp.pad(ids_flat, (0, id_rows * small_width - ids_flat.shape[0]))
    extra_rows = -(-(1 + id_rows) // 16) * 16
    small = jnp.concatenate(
        [
            jnp.concatenate([latent_down, router_proj], axis=1),
            gain_row,
            ids_flat.reshape((id_rows, small_width)),
            jnp.zeros((extra_rows - 1 - id_rows, small_width), BF),
        ],
        axis=0,
    )
    small_four = lax.all_gather(small, "tensor", axis=0, tiled=True)
    tokens_in, _ = lax.optimization_barrier((tokens, small_four))
    rows_all = row_major(lax.all_gather(row_major(tokens_in), "tensor", axis=0, tiled=True))
    small_all = row_major(lax.all_gather(row_major(small_four), "dp", axis=0, tiled=True)).reshape(
        (n_all, down_rows + extra_rows, small_width)
    )
    q_columns, o_columns = query_proj.shape[1], output_proj.shape[1]
    q_rows = query_proj.shape[0]
    heads_mine = jnp.concatenate(
        [query_proj, output_proj, kv_expand.reshape((q_rows, -1))], axis=1
    )
    heads_full = gather_rows(heads_mine, "dp")
    query_full = heads_full[:, :q_columns]
    out_full = heads_full[:, q_columns : q_columns + o_columns]
    expand_full = heads_full[:, q_columns + o_columns :].reshape((-1, kv_expand.shape[1]))
    cot_in, _, _ = lax.optimization_barrier((cotangent, heads_full, small_all))
    cot_all = row_major(lax.all_gather(row_major(cot_in), both, axis=0, tiled=True))
    down_router = small_all[:, :down_rows].reshape((n_all * down_rows, small_width))
    down_full = down_router[:, :lat_rope]
    router_full = down_router[:, lat_rope:]
    gains = small_all[:, down_rows].astype(F32)
    gain_one = gains[:, :gain_piece].reshape(-1)
    gain_two = gains[:, gain_piece : 2 * gain_piece].reshape(-1)
    gain_lat = gains[:, 2 * gain_piece : 2 * gain_piece + lat_piece].reshape(-1)
    ids_all = (
        small_all[:, down_rows + 1 : down_rows + 1 + id_rows]
        .reshape((n_all, id_rows * small_width))[:, : own_rows * TOPK]
        .astype(jnp.int32)
        .reshape((n_dp, count, TOPK))
    )

    first_expert = dp_index * local_experts
    here = first_expert + jnp.arange(local_experts, dtype=jnp.int32)
    named = jnp.any(ids_all[:, None, :, :] == here[None, :, None, None], axis=-1)
    token_pos = jnp.arange(count, dtype=jnp.int32)
    earlier = (token_pos[:, None] < token_pos[None, :]).astype(BF)
    position = lax.dot_general(
        named.astype(BF).reshape((n_dp * local_experts, count)),
        earlier,
        (((1,), (0,)), ((), ())),
        preferred_element_type=F32,
    ).reshape((n_dp, local_experts, count))
    position = jnp.where(named, position, -1.0)
    every = jnp.arange(EXPERTS, dtype=jnp.int32)
    spare = -(-EXPERTS // 128) * 128
    chosen_mask = jnp.any(ids_all[:, :, :, None] == every[None, None, None, :], axis=2).astype(F32)
    mask_wide = jnp.pad(chosen_mask, ((0, 0), (0, 0), (0, spare - EXPERTS)))
    router_wide = jnp.pad(router_full, ((0, 0), (0, spare - EXPERTS)))

    width_q = NOPE + ROPE
    local_heads = query_full.shape[1] // width_q
    cosines, sines = rope_tables(count, ROPE)
    residual = rows_all.astype(F32)
    inv_one = rms_scale(residual)
    normed_one = (residual * inv_one * gain_one).astype(BF)
    latent = jnp.dot(normed_one, down_full, preferred_element_type=F32)
    query = jnp.dot(normed_one, query_full, preferred_element_type=F32).reshape(
        (count, local_heads, width_q)
    )
    compressed = latent[:, :LAT]
    inv_lat = rms_scale(compressed)
    comp_normed = (compressed * inv_lat * gain_lat).astype(BF)
    expanded = jnp.dot(comp_normed, expand_full, preferred_element_type=F32).reshape(
        (count, local_heads, NOPE + VDIM)
    )
    query_rot = rotate(query[:, :, NOPE:], cosines[:, None, :], sines[:, None, :])
    key_rot = rotate(latent[:, LAT:], cosines, sines)
    query_all = jnp.concatenate([query[:, :, :NOPE], query_rot], axis=-1).astype(BF)
    key_all = jnp.concatenate(
        [expanded[:, :, :NOPE], jnp.broadcast_to(key_rot[:, None, :], (count, local_heads, ROPE))],
        axis=-1,
    ).astype(BF)
    value_all = expanded[:, :, NOPE:].astype(BF)
    context, log_total = attend(query_all, key_all, value_all, doc_ids)
    context_b = context.reshape((count, local_heads * VDIM)).astype(BF)
    attn_own = scatter_rows(matmul_t(context_b, out_full), "tensor")
    middle = tokens.astype(F32) + attn_own
    inv_two = rms_scale(middle)
    normed_two_own = (middle * inv_two * gain_two).astype(BF)
    normed_sent, cot_all = lax.optimization_barrier((row_major(normed_two_own), cot_all))
    normed_all = row_major(lax.all_gather(normed_sent, both, axis=0, tiled=True))
    sff = shared_gate.shape[1]
    shared_mine = jnp.concatenate(
        [jnp.transpose(shared_gate), jnp.transpose(shared_up), jnp.transpose(shared_down)], axis=0
    )
    shared_mine, _ = lax.optimization_barrier((shared_mine, normed_all))
    shared_full = lax.all_gather(shared_mine, "dp", axis=1, tiled=True)

    experts_t = jnp.swapaxes(experts, 2, 3)
    first = first_expert.reshape((1,)).astype(jnp.int32)
    grads_disp = dispatch(position, cot_all, capacity)
    rows_disp, slot_w = dispatch_route(
        first, position, normed_all, mask_wide, router_wide, capacity
    )
    out_a, out_b, back_a, back_b, saved = expert_math(
        first, rows_disp, grads_disp, experts_t, slot_w, spare
    )
    half = model_width // 2
    back_a = second_stage(core_stage(position, back_a), "tensor first")
    back_b = second_stage(core_stage(position, back_b), "dp first")
    out_a, out_b, saved, _, _ = lax.optimization_barrier(
        (out_a, out_b, saved, back_a[0], back_b[0])
    )
    grad_experts = jnp.swapaxes(expert_grads(rows_disp, grads_disp, saved), 2, 3)
    out_a = core_stage(position, out_a)
    out_b = core_stage(position, out_b)
    back_a = third_stage(back_a, "tensor first")
    back_b = third_stage(back_b, "dp first")
    back_mark = (back_a[0], back_b[0])
    shared_full, _ = lax.optimization_barrier((shared_full, back_mark))
    sgate_full = shared_full[:sff]
    sup_full = shared_full[sff : 2 * sff]
    sdown_full = shared_full[2 * sff :]
    seq_row = dp_index * count
    normed_two = lax.dynamic_slice_in_dim(normed_all, seq_row, count, 0)
    grad_all = lax.dynamic_slice_in_dim(cot_all, seq_row, count, 0)
    shared_pre_gate = matmul_t(normed_two, sgate_full)
    shared_pre_up = matmul_t(normed_two, sup_full)
    sigma_shared = jax.nn.sigmoid(shared_pre_gate)
    shared_hidden = (shared_pre_gate * sigma_shared * shared_pre_up).astype(BF)
    d_shared = matmul_t(grad_all, sdown_full)
    d_sgate = (
        d_shared * shared_pre_up * sigma_shared * (1.0 + shared_pre_gate * (1.0 - sigma_shared))
    ).astype(BF)
    d_sup = (d_shared * shared_pre_gate * sigma_shared).astype(BF)
    d_shared_part = (dot_nn(d_sgate, sgate_full) + dot_nn(d_sup, sup_full)).astype(BF)
    back_a, back_b, d_shared_part = lax.optimization_barrier((back_a, back_b, d_shared_part))
    d_shared_own = scatter_rows(d_shared_part, "tensor")
    back_own_a, back_own_b = last_stage(back_a), last_stage(back_b)
    shared_own = scatter_rows(dot_nn(shared_hidden, sdown_full), "tensor")
    shared_grads = scatter_products(
        [d_sgate, d_sup, shared_hidden], [normed_two, normed_two, grad_all], "dp"
    )
    own_first = seq_row + first_row
    d_weight = back_own_b[:, half : half + EXPERTS]
    mask_own = lax.dynamic_slice_in_dim(
        chosen_mask.reshape((n_dp * count, EXPERTS)), own_first, own_rows, 0
    )
    scores_own = jax.nn.sigmoid(dot_nn(normed_two_own, router_full))
    chosen_own = scores_own * mask_own
    total_own = jnp.sum(chosen_own, axis=1, keepdims=True)
    d_chosen = route_scale * (
        d_weight / total_own
        - jnp.sum(d_weight * chosen_own, axis=1, keepdims=True) / (total_own * total_own)
    )
    d_logits = (d_chosen * mask_own * scores_own * (1.0 - scores_own)).astype(BF)
    d_normed_two = (
        d_shared_own
        + jnp.concatenate([back_own_a, back_own_b[:, :half]], axis=1)
        + matmul_t(d_logits, router_full)
    )
    grad_gain_two = jnp.sum(d_normed_two * middle * inv_two, axis=0)
    d_middle = cotangent.astype(F32) + norm_back(d_normed_two, middle, inv_two, gain_two)
    two_high, two_low = split_high_low(grad_gain_two)
    mid_sent = jnp.concatenate(
        [
            jnp.concatenate(
                [d_middle.astype(BF), jnp.pad(d_logits, ((0, 0), (0, spare - EXPERTS)))], axis=1
            ),
            jnp.pad(jnp.stack([two_high, two_low]), ((0, 14), (0, spare))),
        ],
        axis=0,
    )
    out_a, out_b, mid_sent = lax.optimization_barrier((out_a, out_b, mid_sent))
    out_a = third_stage(second_stage(out_a, "tensor first"), "tensor first")
    out_b = third_stage(second_stage(out_b, "tensor first"), "tensor first")
    out_own_a, out_own_b = last_stage(out_a), last_stage(out_b)
    block_out = middle + shared_own + jnp.concatenate([out_own_a, out_own_b], axis=1)
    mid_all = gather_rows(row_major(mid_sent), "tensor").reshape(
        (n_tensor, own_rows + 16, model_width + spare)
    )
    d_mid_b = mid_all[:, :own_rows, :model_width].reshape((count, model_width))
    d_logits_seq = mid_all[:, :own_rows, model_width : model_width + EXPERTS].reshape(
        (count, EXPERTS)
    )
    gain_two_sum = jnp.sum(mid_all[:, own_rows : own_rows + 2, :model_width].astype(F32), axis=(0, 1))
    grad_out = scatter_rows(matmul_tl(d_mid_b, context_b), "dp")
    d_context = (
        jnp.dot(d_mid_b, out_full, preferred_element_type=F32)
        .astype(BF)
        .reshape((count, local_heads, VDIM))
    )
    d_query, d_key, d_value = attend_back(
        query_all, key_all, value_all, doc_ids, log_total, d_context
    )
    d_query_rot = unrotate(d_query[:, :, NOPE:], cosines[:, None, :], sines[:, None, :])
    d_query_all = (
        jnp.concatenate([d_query[:, :, :NOPE], d_query_rot], axis=-1)
        .reshape((count, local_heads * width_q))
        .astype(BF)
    )
    d_expanded = (
        jnp.concatenate([d_key[:, :, :NOPE], d_value], axis=-1)
        .reshape((count, local_heads * (NOPE + VDIM)))
        .astype(BF)
    )
    d_key_rot = jnp.sum(d_key[:, :, NOPE:], axis=1)
    back_own = scatter_rows(
        jnp.concatenate(
            [
                matmul_t(d_query_all, query_full).astype(BF),
                matmul_t(d_expanded, expand_full).astype(BF),
                d_key_rot.astype(BF),
                jnp.zeros((count, ROPE), BF),
            ],
            axis=1,
        ),
        "tensor",
    )
    grad_query = scatter_rows(matmul_tl(normed_one, d_query_all), "dp")
    grad_expand = scatter_rows(matmul_tl(comp_normed, d_expanded), "dp")
    d_rows_query = back_own[:, :model_width]
    d_comp_own = back_own[:, model_width : model_width + LAT]
    d_rot_own = back_own[:, model_width + LAT : model_width + LAT + ROPE]
    seq_own = lambda values: lax.dynamic_slice_in_dim(values, first_row, own_rows, 0)
    compressed_own, inv_lat_own = seq_own(compressed), seq_own(inv_lat)
    grad_gain_lat = jnp.sum(d_comp_own * compressed_own * inv_lat_own, axis=0)
    d_comp = norm_back(d_comp_own, compressed_own, inv_lat_own, gain_lat)
    d_latent = jnp.concatenate(
        [d_comp, unrotate(d_rot_own, seq_own(cosines), seq_own(sines))], axis=-1
    ).astype(BF)
    lat_high, lat_low = split_high_low(grad_gain_lat)
    lat_sent = jnp.concatenate(
        [d_latent, jnp.pad(jnp.stack([lat_high, lat_low]), ((0, 14), (0, lat_rope - LAT)))], axis=0
    )
    lat_all = gather_rows(row_major(lat_sent), "tensor").reshape(
        (n_tensor, own_rows + 16, lat_rope)
    )
    d_latent_seq = lat_all[:, :own_rows].reshape((count, lat_rope))
    gain_lat_sum = jnp.sum(lat_all[:, own_rows : own_rows + 2, :LAT].astype(F32), axis=(0, 1))
    residual_own, inv_one_own = tokens.astype(F32), seq_own(inv_one)
    d_normed_one = d_rows_query + matmul_t(d_latent, down_full)
    grad_gain_one = jnp.sum(d_normed_one * residual_own * inv_one_own, axis=0)
    grad_tokens = d_middle + norm_back(d_normed_one, residual_own, inv_one_own, gain_one)
    gain_one_share = scatter_rows(
        jnp.swapaxes(grad_gain_one.reshape((n_dp, n_tensor, gain_piece)), 0, 1), "tensor"
    )[0]

    def own_share(values, piece):
        view = values.reshape((n_dp, n_tensor, piece) + values.shape[1:])
        return pick(view, tensor_index, 1)

    wide = jnp.concatenate(
        [
            own_share(matmul_tl(normed_one, d_latent_seq), down_rows),
            own_share(matmul_tl(normed_two, d_logits_seq), down_rows),
        ],
        axis=2,
    )
    gain_line = jnp.concatenate(
        [gain_one_share, own_share(gain_two_sum, gain_piece), own_share(gain_lat_sum, lat_piece)],
        axis=1,
    )
    gain_line = jnp.pad(
        gain_line[:, None, :], ((0, 0), (0, 15), (0, small_width - 2 * gain_piece - lat_piece))
    )
    small_sum = scatter_rows(
        jnp.concatenate([wide, gain_line], axis=1).reshape((n_dp * (down_rows + 16), small_width)),
        "dp",
    )
    gain_out = small_sum[down_rows]
    return (
        block_out,
        grad_tokens,
        gain_out[:gain_piece],
        gain_out[gain_piece : 2 * gain_piece],
        gain_out[2 * gain_piece : 2 * gain_piece + lat_piece],
        small_sum[:down_rows, :lat_rope],
        small_sum[:down_rows, lat_rope:],
        grad_query,
        grad_expand,
        grad_out,
        jnp.transpose(shared_grads[:sff]),
        jnp.transpose(shared_grads[sff : 2 * sff]),
        jnp.transpose(shared_grads[2 * sff :]),
        grad_experts,
    )


def solution(mesh):
    in_specs = (
        P(("dp", "tensor"), None),
        P("dp", None),
        P("dp", None),
        P(("dp", "tensor"), None),
        P(("dp", "tensor")),
        P(("dp", "tensor")),
        P(("dp", "tensor")),
        P(("dp", "tensor"), None),
        P(("dp", "tensor"), None),
        P("dp", "tensor"),
        P("dp", "tensor"),
        P("dp", "tensor"),
        P("dp", "tensor"),
        P("dp", "tensor"),
        P("dp", "tensor"),
        P("dp", None, None, "tensor"),
    )
    out_specs = (
        P(("dp", "tensor"), None),
        P(("dp", "tensor"), None),
        P(("dp", "tensor")),
        P(("dp", "tensor")),
        P(("dp", "tensor")),
        P(("dp", "tensor"), None),
        P(("dp", "tensor"), None),
        P("dp", "tensor"),
        P("dp", "tensor"),
        P("dp", "tensor"),
        P("dp", "tensor"),
        P("dp", "tensor"),
        P("dp", "tensor"),
        P("dp", None, None, "tensor"),
    )
    return jax.shard_map(body, mesh=mesh, in_specs=in_specs, out_specs=out_specs, check_vma=False)
```

```python
import math

import jax
import jax.numpy as jnp
from jax import lax
from jax.experimental import pallas as pl
from jax.experimental.pallas import tpu as pltpu
from jax.experimental.layout import Layout, with_layout_constraint
from jax.sharding import PartitionSpec as P

NOPE = 128
ROPE = 64
VDIM = 128
LAT = 512
EXPERTS = 64
TOPK = 6


eps = 1e-06
route_scale = 2.446
rope_base = 50000.0


def rms_scale(values):
    return lax.rsqrt(jnp.mean(values * values, axis=-1, keepdims=True) + eps)


def norm_back(grad_normed, values, inverse, gain):
    scaled = grad_normed * gain
    return inverse * scaled - values * inverse * inverse * inverse * jnp.mean(
        scaled * values, axis=-1, keepdims=True
    )


def rope_tables(count, width):
    half = width // 2
    powers = jnp.arange(half, dtype=jnp.int32).astype(jnp.float32) * (2.0 / width)
    freqs = jnp.exp(-math.log(rope_base) * powers)
    angles = jnp.arange(count, dtype=jnp.int32).astype(jnp.float32)[:, None] * freqs[None, :]
    return (jnp.cos(angles), jnp.sin(angles))


def rotate(values, cosines, sines):
    half = values.shape[-1] // 2
    first = values[..., :half]
    second = values[..., half:]
    return jnp.concatenate(
        [first * cosines - second * sines, second * cosines + first * sines], axis=-1
    )


def unrotate(grads, cosines, sines):
    half = grads.shape[-1] // 2
    first = grads[..., :half]
    second = grads[..., half:]
    return jnp.concatenate(
        [first * cosines + second * sines, second * cosines - first * sines], axis=-1
    )


def matmul_t(left, right):
    return lax.dot_general(
        left, right, (((1,), (1,)), ((), ())), preferred_element_type=jnp.float32
    )


def matmul_tl(left, right):
    return lax.dot_general(
        left, right, (((0,), (0,)), ((), ())), preferred_element_type=jnp.float32
    )


def attend(query_all, key_all, value_all, doc_ids):
    count = query_all.shape[0]
    block = min(512, count)
    scale = 1.0 / math.sqrt(query_all.shape[-1])
    key_pos = jnp.arange(count, dtype=jnp.int32)

    def one_block(begin):
        query_pos = begin + jnp.arange(block, dtype=jnp.int32)
        allowed = (doc_ids[:, None] == doc_ids[None, :]) & (key_pos[None, :] <= query_pos[:, None])
        scores = (
            jnp.einsum("qhc,khc->hqk", query_all, key_all, preferred_element_type=jnp.float32)
            * scale
        )
        raw_weights = jnp.where(allowed[None], jnp.exp(scores), 0.0)
        total = jnp.sum(raw_weights, axis=-1)
        probs = (raw_weights / total[..., None]).astype(jnp.bfloat16)
        context = jnp.einsum("hqk,khc->qhc", probs, value_all, preferred_element_type=jnp.float32)
        return (context, jnp.log(total))

    begins = jnp.arange(0, count, block, dtype=jnp.int32)
    contexts, logs = lax.map(one_block, begins)
    heads = query_all.shape[1]
    context = contexts.reshape((count, heads, value_all.shape[2]))
    log_total = jnp.transpose(logs, (1, 0, 2)).reshape((heads, count))
    return (context, log_total)


def attend_back(query_all, key_all, value_all, doc_ids, log_total, d_context):
    count = query_all.shape[0]
    heads = query_all.shape[1]
    block = min(512, count)
    scale = 1.0 / math.sqrt(query_all.shape[-1])
    key_pos = jnp.arange(count, dtype=jnp.int32)

    def one_block(carry, begin):
        d_keys, d_values = carry
        query_pos = begin + jnp.arange(block, dtype=jnp.int32)
        allowed = (doc_ids[:, None] == doc_ids[None, :]) & (key_pos[None, :] <= query_pos[:, None])
        scores = (
            jnp.einsum("qhc,khc->hqk", query_all, key_all, preferred_element_type=jnp.float32)
            * scale
        )
        probs = jnp.where(allowed[None], jnp.exp(scores - log_total[..., None]), 0.0)
        d_values = d_values + jnp.einsum(
            "hqk,qhc->khc",
            probs.astype(jnp.bfloat16),
            d_context,
            preferred_element_type=jnp.float32,
        )
        d_probs = jnp.einsum(
            "qhc,khc->hqk", d_context, value_all, preferred_element_type=jnp.float32
        )
        delta = jnp.sum(probs * d_probs, axis=-1, keepdims=True)
        d_scores = (probs * (d_probs - delta) * scale).astype(jnp.bfloat16)
        d_queries = jnp.einsum(
            "hqk,khc->qhc", d_scores, key_all, preferred_element_type=jnp.float32
        )
        d_keys = d_keys + jnp.einsum(
            "hqk,qhc->khc", d_scores, query_all, preferred_element_type=jnp.float32
        )
        return ((d_keys, d_values), d_queries)

    begins = jnp.arange(0, count, block, dtype=jnp.int32)
    start_state = (jnp.zeros(key_all.shape, jnp.float32), jnp.zeros(value_all.shape, jnp.float32))
    (d_keys, d_values), d_queries = lax.scan(one_block, start_state, begins)
    return (d_queries.reshape((count, heads, query_all.shape[2])), d_keys, d_values)


BF = jnp.bfloat16
F32 = jnp.float32


def row_major(array):
    return with_layout_constraint(array, Layout(major_to_minor=tuple(range(array.ndim))))


def factor_pairs(size, stride, parts, shift):
    pairs = []
    for index in range(size):
        place = index // stride % parts
        pairs.append((index, index + ((place + shift) % parts - place) * stride))
    return pairs


def pick(array, index, dim):
    return lax.dynamic_index_in_dim(array, index, dim, keepdims=False)


def scatter_factor(array, dim, axis, stride, parts, final=False):
    size = lax.axis_size(axis)
    place = lax.axis_index(axis) // stride % parts
    received = [
        lax.ppermute(
            pick(array, (place + shift) % parts, dim),
            axis,
            factor_pairs(size, stride, parts, shift),
        )
        for shift in range(1, parts)
    ]
    total = pick(array, place, dim).astype(F32)
    for item in received:
        total = total + item.astype(F32)
    return total if final else total.astype(BF)


def factors(axis):
    size = lax.axis_size(axis)
    inner = 2 if size % 2 == 0 else 1
    return size // inner, inner


def gather_pieces(shard, axis, before=None):
    size = lax.axis_size(axis)
    outer, inner = factors(axis)
    index = lax.axis_index(axis)
    far, near = index // inner, index % inner
    pieces = [shard] + [
        lax.ppermute(shard, axis, factor_pairs(size, inner, outer, shift))
        for shift in range(1, outer)
    ]
    if before is not None:
        pieces[0], _ = lax.optimization_barrier((pieces[0], before))
        pieces[-1], _ = lax.optimization_barrier((pieces[-1], before))
    found = []
    for shift, piece in enumerate(pieces):
        source = (far - shift) % outer
        found.append((source, near, piece))
        for turn in range(1, inner):
            other = lax.ppermute(piece, axis, factor_pairs(size, 1, inner, turn))
            found.append((source, (near - turn) % inner, other))
    return found


def gather_rows(shard, axis, before=None):
    inner = factors(axis)[1]
    rows = shard.shape[0]
    full = jnp.zeros((lax.axis_size(axis) * rows,) + shard.shape[1:], shard.dtype)
    rest = (0,) * (shard.ndim - 1)
    for far, near, piece in gather_pieces(shard, axis, before):
        full = lax.dynamic_update_slice(full, piece, ((far * inner + near) * rows,) + rest)
    return full


def scatter_rows(array, axis, final=True):
    outer, inner = factors(axis)
    rows = array.shape[0] // (outer * inner)
    view = row_major(array.astype(BF)).reshape((outer, inner, rows) + array.shape[1:])
    view = scatter_factor(view, 1, axis, 1, inner)
    return scatter_factor(view, 0, axis, inner, outer, final)


def scatter_products(lefts, rights, axis):
    size = lax.axis_size(axis)
    blocks = jnp.concatenate(
        [matmul_tl(left, right).astype(BF) for left, right in zip(lefts, rights)], axis=0
    )
    rows, columns = blocks.shape[0], blocks.shape[1] // size
    blocks = jnp.swapaxes(blocks.reshape((rows, size, columns)), 0, 1)
    blocks = row_major(blocks.reshape((size * rows, columns)))
    return lax.psum_scatter(blocks, axis, scatter_dimension=0, tiled=True).astype(F32)


def dot_nn(left, right):
    return lax.dot_general(left, right, (((1,), (0,)), ((), ())), preferred_element_type=F32)


def place_of(position_ref, capacity):
    _, count, tokens = position_ref.shape
    slot = lax.broadcasted_iota(jnp.int32, (capacity, tokens), 0).astype(F32)
    return jnp.concatenate(
        [
            jnp.where(position_ref[0, e : e + 1, :] == slot, 1.0, 0.0).astype(BF)
            for e in range(count)
        ],
        axis=0,
    )


def dispatch_kernel(position_ref, rows_ref, out_ref):
    place = place_of(position_ref, out_ref.shape[2])
    out_ref[...] = dot_nn(place, rows_ref[0]).astype(BF).reshape(out_ref.shape)


def route_kernel(first_ref, position_ref, rows_ref, mask_ref, router_ref, out_ref, slot_w_ref):
    _, count, capacity, width = out_ref.shape
    place = place_of(position_ref, capacity)
    rows = rows_ref[0]
    out_ref[...] = dot_nn(place, rows).astype(BF).reshape(out_ref.shape)
    chosen = jax.nn.sigmoid(dot_nn(rows, router_ref[...])) * mask_ref[0]
    weights = route_scale * chosen / jnp.sum(chosen, axis=1, keepdims=True)
    high = weights.astype(BF)
    low = (weights - high.astype(F32)).astype(BF)
    spread = dot_nn(place, high) + dot_nn(place, low)
    lane = lax.broadcasted_iota(jnp.int32, spread.shape, 1)
    slot_expert = lax.broadcasted_iota(jnp.int32, spread.shape, 0) // capacity + first_ref[0]
    mine = jnp.sum(jnp.where(lane == slot_expert, spread, 0.0), axis=1, keepdims=True)
    slot_w_ref[...] = jnp.broadcast_to(mine, spread.shape).reshape(slot_w_ref.shape)


def dispatch(position, rows, capacity):
    groups, count, tokens = position.shape
    width = rows.shape[1]
    return pl.pallas_call(
        dispatch_kernel,
        grid=(groups,),
        in_specs=[
            pl.BlockSpec((1, count, tokens), lambda s: (s, 0, 0)),
            pl.BlockSpec((1, tokens, width), lambda s: (s, 0, 0)),
        ],
        out_specs=pl.BlockSpec((1, count, capacity, width), lambda s: (s, 0, 0, 0)),
        out_shape=jax.ShapeDtypeStruct((groups, count, capacity, width), BF),
        name="dispatch",
    )(position, rows.reshape((groups, tokens, width)))


def dispatch_route(first, position, rows, mask, router, capacity):
    groups, count, tokens = position.shape
    width = rows.shape[1]
    lanes = router.shape[1]
    slab = lambda cols: pl.BlockSpec((1, count, capacity, cols), lambda s, _: (s, 0, 0, 0))
    return pl.pallas_call(
        route_kernel,
        grid_spec=pltpu.PrefetchScalarGridSpec(
            num_scalar_prefetch=1,
            grid=(groups,),
            in_specs=[
                pl.BlockSpec((1, count, tokens), lambda s, _: (s, 0, 0)),
                pl.BlockSpec((1, tokens, width), lambda s, _: (s, 0, 0)),
                pl.BlockSpec((1, tokens, lanes), lambda s, _: (s, 0, 0)),
                pl.BlockSpec((width, lanes), lambda s, _: (0, 0)),
            ],
            out_specs=[slab(width), slab(lanes)],
        ),
        out_shape=[
            jax.ShapeDtypeStruct((groups, count, capacity, width), BF),
            jax.ShapeDtypeStruct((groups, count, capacity, lanes), F32),
        ],
        name="dispatch_route",
    )(first, position, rows.reshape((groups, tokens, width)), mask, router)


def expert_kernel(
    first_ref, rows_ref, grads_ref, weights_ref, slot_w_ref,
    out_a_ref, out_b_ref, back_a_ref, back_b_ref, saved_ref,
):
    groups, _, capacity, width = rows_ref.shape
    slots = groups * capacity
    rows = rows_ref[...].reshape((slots, width))
    grads = grads_ref[...].reshape((slots, width))
    gate = matmul_t(rows, weights_ref[0, 0])
    up = matmul_t(rows, weights_ref[0, 1])
    d_plain = matmul_t(grads, weights_ref[0, 2])
    slot_w = slot_w_ref[...].reshape((slots, slot_w_ref.shape[-1]))[:, :1]
    sigma = jax.nn.sigmoid(gate)
    silu = gate * sigma
    hidden = silu * up
    d_weight = jnp.sum(hidden * d_plain, axis=1, keepdims=True)
    hidden_w = (hidden * slot_w).astype(BF)
    d_hidden = d_plain * slot_w
    d_gate = (d_hidden * up * sigma * (1.0 + gate * (1.0 - sigma))).astype(BF)
    d_up = (d_hidden * silu).astype(BF)
    saved_ref[0, 0] = d_gate
    saved_ref[0, 1] = d_up
    saved_ref[0, 2] = hidden_w
    half = out_a_ref.shape[-1]
    shape_half = (groups, 1, capacity, half)
    for part, out_ref, back_ref in ((0, out_a_ref, back_a_ref), (1, out_b_ref, back_b_ref)):
        cols = pl.ds(part * half, half)
        back = dot_nn(d_gate, weights_ref[0, 0, :, cols]) + dot_nn(
            d_up, weights_ref[0, 1, :, cols]
        )
        back_ref[:, :, :, :half] = back.astype(BF).reshape(shape_half)
        out_ref[...] = dot_nn(hidden_w, weights_ref[0, 2, :, cols]).astype(BF).reshape(shape_half)
    spare = back_b_ref.shape[-1] - half
    lane = lax.broadcasted_iota(jnp.int32, (slots, spare), 1)
    spread = jnp.where(lane == first_ref[0] + pl.program_id(0), d_weight, 0.0)
    back_b_ref[:, :, :, half:] = spread.astype(BF).reshape((groups, 1, capacity, spare))


def group_tile(groups, capacity):
    return max(t for t in range(1, groups + 1) if groups % t == 0 and t * capacity <= 512)


def expert_math(first, rows, grads, experts_t, slot_w, spare):
    groups, count, capacity, width = rows.shape
    hidden = experts_t.shape[2]
    tile = group_tile(groups, capacity)
    half = width // 2
    slab = lambda cols: pl.BlockSpec((tile, 1, capacity, cols), lambda e, s, _: (s, e, 0, 0))
    shape = lambda cols: jax.ShapeDtypeStruct((groups, count, capacity, cols), BF)
    slots = groups * capacity
    return pl.pallas_call(
        expert_kernel,
        grid_spec=pltpu.PrefetchScalarGridSpec(
            num_scalar_prefetch=1,
            grid=(count, groups // tile),
            in_specs=[
                slab(width),
                slab(width),
                pl.BlockSpec((1, 3, hidden, width), lambda e, s, _: (e, 0, 0, 0)),
                slab(slot_w.shape[-1]),
            ],
            out_specs=[
                slab(half),
                slab(half),
                slab(half),
                slab(half + spare),
                pl.BlockSpec((1, 3, tile * capacity, hidden), lambda e, s, _: (e, 0, s, 0)),
            ],
        ),
        out_shape=[
            shape(half),
            shape(half),
            shape(half),
            shape(half + spare),
            jax.ShapeDtypeStruct((count, 3, slots, hidden), BF),
        ],
        compiler_params=pltpu.CompilerParams(vmem_limit_bytes=60 * 1024 * 1024),
        name="expert_math",
    )(first, rows, grads, experts_t, slot_w)


def expert_grad_kernel(rows_ref, grads_ref, saved_ref, out_ref):
    groups, _, capacity, width = rows_ref.shape
    slots = groups * capacity
    rows = rows_ref[...].reshape((slots, width))
    grads = grads_ref[...].reshape((slots, width))
    found = (
        matmul_tl(saved_ref[0, 0], rows),
        matmul_tl(saved_ref[0, 1], rows),
        matmul_tl(saved_ref[0, 2], grads),
    )

    @pl.when(pl.program_id(1) == 0)
    def _():
        for which in range(3):
            out_ref[0, which] = found[which]

    @pl.when(pl.program_id(1) > 0)
    def _():
        for which in range(3):
            out_ref[0, which] += found[which]


def expert_grads(rows, grads, saved):
    groups, count, capacity, width = rows.shape
    hidden = saved.shape[3]
    tile = group_tile(groups, capacity)
    slab = pl.BlockSpec((tile, 1, capacity, width), lambda e, s: (s, e, 0, 0))
    return pl.pallas_call(
        expert_grad_kernel,
        grid=(count, groups // tile),
        in_specs=[
            slab,
            slab,
            pl.BlockSpec((1, 3, tile * capacity, hidden), lambda e, s: (e, 0, s, 0)),
        ],
        out_specs=pl.BlockSpec((1, 3, hidden, width), lambda e, s: (e, 0, 0, 0)),
        out_shape=jax.ShapeDtypeStruct((count, 3, hidden, width), F32),
        compiler_params=pltpu.CompilerParams(vmem_limit_bytes=60 * 1024 * 1024),
        name="expert_grads",
    )(rows, grads, saved)


def combine_kernel(core_ref, position_ref, values_ref, keep_ref, send_ref):
    _, count, capacity, width = values_ref.shape
    tokens = position_ref.shape[2]
    own = tokens // (2 * keep_ref.shape[1])
    place = place_of(position_ref, capacity)
    found = matmul_tl(place, values_ref[...].reshape((count * capacity, width))).astype(BF)
    found = found.reshape((keep_ref.shape[1], 2, own, width))
    for core in range(2):

        @pl.when(core_ref[0] == core)
        def _():
            keep_ref[0] = found[:, core]
            send_ref[0] = found[:, 1 - core]


def core_stage(position, values):
    groups, count, tokens = position.shape
    capacity, width = values.shape[2:]
    size = lax.axis_size("tensor")
    outer, inner = factors("tensor")
    own = tokens // size
    core = lax.axis_index("tensor") % inner
    slab = pl.BlockSpec((1, outer, own, width), lambda s, _: (s, 0, 0, 0))
    shape = jax.ShapeDtypeStruct((groups, outer, own, width), BF)
    keep, send = pl.pallas_call(
        combine_kernel,
        grid_spec=pltpu.PrefetchScalarGridSpec(
            num_scalar_prefetch=1,
            grid=(groups,),
            in_specs=[
                pl.BlockSpec((1, count, tokens), lambda s, _: (s, 0, 0)),
                pl.BlockSpec((1, count, capacity, width), lambda s, _: (s, 0, 0, 0)),
            ],
            out_specs=[slab, slab],
        ),
        out_shape=[shape, shape],
        name="combine",
    )(core.reshape((1,)).astype(jnp.int32), position, values)
    return [keep, lax.ppermute(send, "tensor", factor_pairs(size, 1, inner, 1))]


def sum_split_kernel(count, place_ref, *refs):
    parts = refs[0].shape[1]
    for shift, out_ref in enumerate(refs[count:]):
        index = lax.rem(place_ref[0] + shift, parts)
        total = refs[0][0, index].astype(F32)
        for ref in refs[1:count]:
            total = total + ref[0, index].astype(F32)
        out_ref[0] = total.astype(BF)


def stage(arrays, lead, axis, stride, parts):
    width = arrays[0].shape[-1]
    size = lax.axis_size(axis)
    place = lax.axis_index(axis) // stride % parts
    rows = arrays[0].size // (lead * parts * width)
    views = [array.reshape((lead, parts, rows, width)) for array in arrays]
    tile = 32 if rows % 32 == 0 else rows
    if parts * rows * width * (len(views) + 1) <= 4 << 20:
        tile = rows
    found = pl.pallas_call(
        lambda *refs: sum_split_kernel(len(views), *refs),
        grid_spec=pltpu.PrefetchScalarGridSpec(
            num_scalar_prefetch=1,
            grid=(lead, rows // tile),
            in_specs=[pl.BlockSpec((1, parts, tile, width), lambda a, r, _: (a, 0, r, 0))]
            * len(views),
            out_specs=[pl.BlockSpec((1, tile, width), lambda a, r, _: (a, r, 0))] * parts,
        ),
        out_shape=[jax.ShapeDtypeStruct((lead, rows, width), BF)] * parts,
        name="sum_split",
    )(place.reshape((1,)).astype(jnp.int32), *views)
    return [found[0]] + [
        lax.ppermute(found[shift], axis, factor_pairs(size, stride, parts, shift))
        for shift in range(1, parts)
    ]


def second_stage(arrays, order):
    groups, outer = arrays[0].shape[:2]
    inner = factors("tensor")[1]
    far, near = factors("dp")
    if order == "tensor first":
        return stage(arrays, groups, "tensor", inner, outer)
    return stage(arrays, far, "dp", 1, near)


def third_stage(arrays, order):
    outer, inner = factors("tensor")
    far, near = factors("dp")
    if order == "tensor first":
        return stage(arrays, far, "dp", 1, near)
    return stage(arrays, far, "tensor", inner, outer)


def last_stage(arrays):
    far, near = factors("dp")
    return stage(arrays, 1, "dp", near, far)


def last_sum(arrays):
    total = arrays[0][0].astype(F32)
    for item in arrays[1:]:
        total = total + item[0].astype(F32)
    return total


def split_high_low(values):
    high = values.astype(BF)
    return high, (values - high.astype(F32)).astype(BF)


def body(
    tokens,
    segments,
    expert_ids,
    cotangent,
    attn_gain,
    ffn_gain,
    latent_gain,
    latent_down,
    router_proj,
    query_proj,
    kv_expand,
    output_proj,
    shared_gate,
    shared_up,
    shared_down,
    experts,
):
    both = ("dp", "tensor")
    n_dp, n_tensor = lax.axis_size("dp"), lax.axis_size("tensor")
    n_all = n_dp * n_tensor
    dp_index, tensor_index = lax.axis_index("dp"), lax.axis_index("tensor")
    own_rows, model_width = tokens.shape
    count = own_rows * n_tensor
    first_row = tensor_index * own_rows
    down_rows, lat_rope = latent_down.shape
    local_experts = experts.shape[0]
    capacity = count * TOPK * 4 // (3 * EXPERTS)
    slots = local_experts * capacity
    doc_ids = segments[0]

    small_width = lat_rope + EXPERTS
    own_ids = lax.dynamic_slice_in_dim(expert_ids, first_row, own_rows, 0)
    gain_piece, lat_piece = attn_gain.shape[0], latent_gain.shape[0]
    gain_row = jnp.concatenate([attn_gain, ffn_gain, latent_gain])
    gain_row = jnp.pad(gain_row, (0, small_width - gain_row.shape[0]))[None]
    id_rows = -(-own_rows * TOPK // small_width)
    ids_flat = own_ids.astype(BF).reshape(-1)
    ids_flat = jnp.pad(ids_flat, (0, id_rows * small_width - ids_flat.shape[0]))
    extra_rows = -(-(1 + id_rows) // 16) * 16
    small = jnp.concatenate(
        [
            jnp.concatenate([latent_down, router_proj], axis=1),
            gain_row,
            ids_flat.reshape((id_rows, small_width)),
            jnp.zeros((extra_rows - 1 - id_rows, small_width), BF),
        ],
        axis=0,
    )
    small_four = lax.all_gather(small, "tensor", axis=0, tiled=True)
    rows_all = gather_rows(tokens, "tensor")
    small_all = row_major(lax.all_gather(row_major(small_four), "dp", axis=0, tiled=True)).reshape(
        (n_all, down_rows + extra_rows, small_width)
    )
    q_columns, o_columns = query_proj.shape[1], output_proj.shape[1]
    q_rows = query_proj.shape[0]
    heads_mine = jnp.concatenate(
        [query_proj, output_proj, kv_expand.reshape((q_rows, -1))], axis=1
    )
    heads_full = gather_rows(heads_mine, "dp", rows_all)
    query_full = heads_full[:, :q_columns]
    out_full = heads_full[:, q_columns : q_columns + o_columns]
    expand_full = heads_full[:, q_columns + o_columns :].reshape((-1, kv_expand.shape[1]))
    cot_in, _, _ = lax.optimization_barrier((cotangent, heads_full, small_all))
    cot_all = row_major(lax.all_gather(row_major(cot_in), both, axis=0, tiled=True))
    down_router = small_all[:, :down_rows].reshape((n_all * down_rows, small_width))
    down_full = down_router[:, :lat_rope]
    router_full = down_router[:, lat_rope:]
    gains = small_all[:, down_rows].astype(F32)
    gain_one = gains[:, :gain_piece].reshape(-1)
    gain_two = gains[:, gain_piece : 2 * gain_piece].reshape(-1)
    gain_lat = gains[:, 2 * gain_piece : 2 * gain_piece + lat_piece].reshape(-1)
    ids_all = (
        small_all[:, down_rows + 1 : down_rows + 1 + id_rows]
        .reshape((n_all, id_rows * small_width))[:, : own_rows * TOPK]
        .astype(jnp.int32)
        .reshape((n_dp, count, TOPK))
    )

    first_expert = dp_index * local_experts
    here = first_expert + jnp.arange(local_experts, dtype=jnp.int32)
    named = jnp.any(ids_all[:, None, :, :] == here[None, :, None, None], axis=-1)
    token_pos = jnp.arange(count, dtype=jnp.int32)
    earlier = (token_pos[:, None] < token_pos[None, :]).astype(BF)
    position = lax.dot_general(
        named.astype(BF).reshape((n_dp * local_experts, count)),
        earlier,
        (((1,), (0,)), ((), ())),
        preferred_element_type=F32,
    ).reshape((n_dp, local_experts, count))
    position = jnp.where(named, position, -1.0)
    every = jnp.arange(EXPERTS, dtype=jnp.int32)
    spare = -(-EXPERTS // 128) * 128
    chosen_mask = jnp.any(ids_all[:, :, :, None] == every[None, None, None, :], axis=2).astype(F32)
    mask_wide = jnp.pad(chosen_mask, ((0, 0), (0, 0), (0, spare - EXPERTS)))
    router_wide = jnp.pad(router_full, ((0, 0), (0, spare - EXPERTS)))

    width_q = NOPE + ROPE
    local_heads = query_full.shape[1] // width_q
    cosines, sines = rope_tables(count, ROPE)
    residual = rows_all.astype(F32)
    inv_one = rms_scale(residual)
    normed_one = (residual * inv_one * gain_one).astype(BF)
    latent = jnp.dot(normed_one, down_full, preferred_element_type=F32)
    query = jnp.dot(normed_one, query_full, preferred_element_type=F32).reshape(
        (count, local_heads, width_q)
    )
    compressed = latent[:, :LAT]
    inv_lat = rms_scale(compressed)
    comp_normed = (compressed * inv_lat * gain_lat).astype(BF)
    expanded = jnp.dot(comp_normed, expand_full, preferred_element_type=F32).reshape(
        (count, local_heads, NOPE + VDIM)
    )
    query_rot = rotate(query[:, :, NOPE:], cosines[:, None, :], sines[:, None, :])
    key_rot = rotate(latent[:, LAT:], cosines, sines)
    query_all = jnp.concatenate([query[:, :, :NOPE], query_rot], axis=-1).astype(BF)
    key_all = jnp.concatenate(
        [expanded[:, :, :NOPE], jnp.broadcast_to(key_rot[:, None, :], (count, local_heads, ROPE))],
        axis=-1,
    ).astype(BF)
    value_all = expanded[:, :, NOPE:].astype(BF)
    context, log_total = attend(query_all, key_all, value_all, doc_ids)
    context_b = context.reshape((count, local_heads * VDIM)).astype(BF)
    attn_own = scatter_rows(matmul_t(context_b, out_full), "tensor")
    middle = tokens.astype(F32) + attn_own
    inv_two = rms_scale(middle)
    normed_two_own = (middle * inv_two * gain_two).astype(BF)
    normed_sent, cot_all, position, mask_wide, router_wide = lax.optimization_barrier(
        (row_major(normed_two_own), cot_all, position, mask_wide, router_wide)
    )
    normed_all = row_major(lax.all_gather(normed_sent, both, axis=0, tiled=True))
    sff = shared_gate.shape[1]
    shared_mine = jnp.concatenate(
        [jnp.transpose(shared_gate), jnp.transpose(shared_up), jnp.transpose(shared_down)], axis=0
    )
    shared_mine, _ = lax.optimization_barrier((shared_mine, normed_all))
    shared_full = lax.all_gather(shared_mine, "dp", axis=1, tiled=True)

    experts_t = jnp.swapaxes(experts, 2, 3)
    first = first_expert.reshape((1,)).astype(jnp.int32)
    grads_disp = dispatch(position, cot_all, capacity)
    rows_disp, slot_w = dispatch_route(
        first, position, normed_all, mask_wide, router_wide, capacity
    )
    out_a, out_b, back_a, back_b, saved = expert_math(
        first, rows_disp, grads_disp, experts_t, slot_w, spare
    )
    half = model_width // 2
    back_a = second_stage(core_stage(position, back_a), "tensor first")
    back_b = second_stage(core_stage(position, back_b), "dp first")
    out_a, out_b, _, _ = lax.optimization_barrier((out_a, out_b, back_a[0], back_b[0]))
    out_a = core_stage(position, out_a)
    out_b = core_stage(position, out_b)
    back_a = third_stage(back_a, "tensor first")
    back_b = third_stage(back_b, "dp first")
    back_mark = (back_a[0], back_b[0])
    shared_full, _ = lax.optimization_barrier((shared_full, back_mark))
    sgate_full = shared_full[:sff]
    sup_full = shared_full[sff : 2 * sff]
    sdown_full = shared_full[2 * sff :]
    seq_row = dp_index * count
    normed_two = lax.dynamic_slice_in_dim(normed_all, seq_row, count, 0)
    grad_all = lax.dynamic_slice_in_dim(cot_all, seq_row, count, 0)
    shared_pre_gate = matmul_t(normed_two, sgate_full)
    shared_pre_up = matmul_t(normed_two, sup_full)
    sigma_shared = jax.nn.sigmoid(shared_pre_gate)
    shared_hidden = (shared_pre_gate * sigma_shared * shared_pre_up).astype(BF)
    d_shared = matmul_t(grad_all, sdown_full)
    d_sgate = (
        d_shared * shared_pre_up * sigma_shared * (1.0 + shared_pre_gate * (1.0 - sigma_shared))
    ).astype(BF)
    d_sup = (d_shared * shared_pre_gate * sigma_shared).astype(BF)
    d_shared_part = (dot_nn(d_sgate, sgate_full) + dot_nn(d_sup, sup_full)).astype(BF)
    back_a, back_b, d_shared_part = lax.optimization_barrier((back_a, back_b, d_shared_part))
    d_shared_own = scatter_rows(d_shared_part, "tensor")
    back_a, back_b = last_stage(back_a), last_stage(back_b)
    saved, _, _ = lax.optimization_barrier((saved, back_a[0], back_b[0]))
    grad_experts = expert_grads(rows_disp, grads_disp, saved)
    back_a, back_b, grad_experts = lax.optimization_barrier((back_a, back_b, grad_experts))
    grad_experts = jnp.swapaxes(grad_experts, 2, 3)
    back_own_a, back_own_b = last_sum(back_a), last_sum(back_b)
    shared_own = scatter_rows(dot_nn(shared_hidden, sdown_full), "tensor")
    shared_grads = scatter_products(
        [d_sgate, d_sup, shared_hidden], [normed_two, normed_two, grad_all], "dp"
    )
    own_first = seq_row + first_row
    d_weight = back_own_b[:, half : half + EXPERTS]
    mask_own = lax.dynamic_slice_in_dim(
        chosen_mask.reshape((n_dp * count, EXPERTS)), own_first, own_rows, 0
    )
    scores_own = jax.nn.sigmoid(dot_nn(normed_two_own, router_full))
    chosen_own = scores_own * mask_own
    total_own = jnp.sum(chosen_own, axis=1, keepdims=True)
    d_chosen = route_scale * (
        d_weight / total_own
        - jnp.sum(d_weight * chosen_own, axis=1, keepdims=True) / (total_own * total_own)
    )
    d_logits = (d_chosen * mask_own * scores_own * (1.0 - scores_own)).astype(BF)
    d_normed_two = (
        d_shared_own
        + jnp.concatenate([back_own_a, back_own_b[:, :half]], axis=1)
        + matmul_t(d_logits, router_full)
    )
    grad_gain_two = jnp.sum(d_normed_two * middle * inv_two, axis=0)
    d_middle = cotangent.astype(F32) + norm_back(d_normed_two, middle, inv_two, gain_two)
    two_high, two_low = split_high_low(grad_gain_two)
    mid_sent = jnp.concatenate(
        [
            jnp.concatenate(
                [d_middle.astype(BF), jnp.pad(d_logits, ((0, 0), (0, spare - EXPERTS)))], axis=1
            ),
            jnp.pad(jnp.stack([two_high, two_low]), ((0, 14), (0, spare))),
        ],
        axis=0,
    )
    out_a, out_b, mid_sent = lax.optimization_barrier((out_a, out_b, mid_sent))
    out_a = third_stage(second_stage(out_a, "tensor first"), "tensor first")
    out_b = third_stage(second_stage(out_b, "tensor first"), "tensor first")
    out_own_a, out_own_b = last_sum(last_stage(out_a)), last_sum(last_stage(out_b))
    block_out = middle + shared_own + jnp.concatenate([out_own_a, out_own_b], axis=1)
    mid_all = gather_rows(row_major(mid_sent), "tensor").reshape(
        (n_tensor, own_rows + 16, model_width + spare)
    )
    d_mid_b = mid_all[:, :own_rows, :model_width].reshape((count, model_width))
    d_logits_seq = mid_all[:, :own_rows, model_width : model_width + EXPERTS].reshape(
        (count, EXPERTS)
    )
    gain_two_sum = jnp.sum(mid_all[:, own_rows : own_rows + 2, :model_width].astype(F32), axis=(0, 1))
    d_context = (
        jnp.dot(d_mid_b, out_full, preferred_element_type=F32)
        .astype(BF)
        .reshape((count, local_heads, VDIM))
    )
    d_query, d_key, d_value = attend_back(
        query_all, key_all, value_all, doc_ids, log_total, d_context
    )
    d_query_rot = unrotate(d_query[:, :, NOPE:], cosines[:, None, :], sines[:, None, :])
    d_query_all = (
        jnp.concatenate([d_query[:, :, :NOPE], d_query_rot], axis=-1)
        .reshape((count, local_heads * width_q))
        .astype(BF)
    )
    d_expanded = (
        jnp.concatenate([d_key[:, :, :NOPE], d_value], axis=-1)
        .reshape((count, local_heads * (NOPE + VDIM)))
        .astype(BF)
    )
    d_key_rot = jnp.sum(d_key[:, :, NOPE:], axis=1)
    outer, inner = factors("tensor")
    back_parts = row_major(
        jnp.concatenate(
            [
                matmul_t(d_query_all, query_full).astype(BF),
                matmul_t(d_expanded, expand_full).astype(BF),
                d_key_rot.astype(BF),
                jnp.zeros((count, ROPE), BF),
            ],
            axis=1,
        )
    ).reshape((outer, inner, own_rows, -1))
    back_parts = scatter_factor(back_parts, 1, "tensor", 1, inner)
    d_query_all, d_expanded, d_mid_b, back_parts = lax.optimization_barrier(
        (d_query_all, d_expanded, d_mid_b, back_parts)
    )
    grad_out = scatter_rows(matmul_tl(d_mid_b, context_b), "dp")
    back_own = scatter_factor(back_parts, 0, "tensor", inner, outer, True)
    grad_query = scatter_rows(matmul_tl(normed_one, d_query_all), "dp")
    grad_expand = scatter_rows(matmul_tl(comp_normed, d_expanded), "dp")
    d_rows_query = back_own[:, :model_width]
    d_comp_own = back_own[:, model_width : model_width + LAT]
    d_rot_own = back_own[:, model_width + LAT : model_width + LAT + ROPE]
    seq_own = lambda values: lax.dynamic_slice_in_dim(values, first_row, own_rows, 0)
    compressed_own, inv_lat_own = seq_own(compressed), seq_own(inv_lat)
    grad_gain_lat = jnp.sum(d_comp_own * compressed_own * inv_lat_own, axis=0)
    d_comp = norm_back(d_comp_own, compressed_own, inv_lat_own, gain_lat)
    d_latent = jnp.concatenate(
        [d_comp, unrotate(d_rot_own, seq_own(cosines), seq_own(sines))], axis=-1
    ).astype(BF)
    lat_high, lat_low = split_high_low(grad_gain_lat)
    lat_sent = jnp.concatenate(
        [d_latent, jnp.pad(jnp.stack([lat_high, lat_low]), ((0, 14), (0, lat_rope - LAT)))], axis=0
    )
    lat_all = gather_rows(row_major(lat_sent), "tensor").reshape(
        (n_tensor, own_rows + 16, lat_rope)
    )
    d_latent_seq = lat_all[:, :own_rows].reshape((count, lat_rope))
    gain_lat_sum = jnp.sum(lat_all[:, own_rows : own_rows + 2, :LAT].astype(F32), axis=(0, 1))
    residual_own, inv_one_own = tokens.astype(F32), seq_own(inv_one)
    d_normed_one = d_rows_query + matmul_t(d_latent, down_full)
    grad_gain_one = jnp.sum(d_normed_one * residual_own * inv_one_own, axis=0)
    grad_tokens = d_middle + norm_back(d_normed_one, residual_own, inv_one_own, gain_one)
    gain_one_share = scatter_rows(
        jnp.swapaxes(grad_gain_one.reshape((n_dp, n_tensor, gain_piece)), 0, 1), "tensor"
    )[0]

    def own_share(values, piece):
        view = values.reshape((n_dp, n_tensor, piece) + values.shape[1:])
        return pick(view, tensor_index, 1)

    wide = jnp.concatenate(
        [
            own_share(matmul_tl(normed_one, d_latent_seq), down_rows),
            own_share(matmul_tl(normed_two, d_logits_seq), down_rows),
        ],
        axis=2,
    )
    gain_line = jnp.concatenate(
        [gain_one_share, own_share(gain_two_sum, gain_piece), own_share(gain_lat_sum, lat_piece)],
        axis=1,
    )
    gain_line = jnp.pad(
        gain_line[:, None, :], ((0, 0), (0, 15), (0, small_width - 2 * gain_piece - lat_piece))
    )
    small_sum = scatter_rows(
        jnp.concatenate([wide, gain_line], axis=1).reshape((n_dp * (down_rows + 16), small_width)),
        "dp",
    )
    gain_out = small_sum[down_rows]
    return (
        block_out,
        grad_tokens,
        gain_out[:gain_piece],
        gain_out[gain_piece : 2 * gain_piece],
        gain_out[2 * gain_piece : 2 * gain_piece + lat_piece],
        small_sum[:down_rows, :lat_rope],
        small_sum[:down_rows, lat_rope:],
        grad_query,
        grad_expand,
        grad_out,
        jnp.transpose(shared_grads[:sff]),
        jnp.transpose(shared_grads[sff : 2 * sff]),
        jnp.transpose(shared_grads[2 * sff :]),
        grad_experts,
    )


def solution(mesh):
    in_specs = (
        P(("dp", "tensor"), None),
        P("dp", None),
        P("dp", None),
        P(("dp", "tensor"), None),
        P(("dp", "tensor")),
        P(("dp", "tensor")),
        P(("dp", "tensor")),
        P(("dp", "tensor"), None),
        P(("dp", "tensor"), None),
        P("dp", "tensor"),
        P("dp", "tensor"),
        P("dp", "tensor"),
        P("dp", "tensor"),
        P("dp", "tensor"),
        P("dp", "tensor"),
        P("dp", None, None, "tensor"),
    )
    out_specs = (
        P(("dp", "tensor"), None),
        P(("dp", "tensor"), None),
        P(("dp", "tensor")),
        P(("dp", "tensor")),
        P(("dp", "tensor")),
        P(("dp", "tensor"), None),
        P(("dp", "tensor"), None),
        P("dp", "tensor"),
        P("dp", "tensor"),
        P("dp", "tensor"),
        P("dp", "tensor"),
        P("dp", "tensor"),
        P("dp", "tensor"),
        P("dp", None, None, "tensor"),
    )
    return jax.shard_map(body, mesh=mesh, in_specs=in_specs, out_specs=out_specs, check_vma=False)
```
